256 devices in a mesh: slab: 32 (over z_hi, x, y), pencil: 8 (over z_lo, core).
Axes of the slice: x: 4, y: 4, z: 8 (z_hi: 2, z_lo: 4; z = z_hi * 4 + z_lo), core: 2. Of those that a mesh axis runs over, the one named last changes fastest.
Arguments:
- adjoint_vort: float32 [3, 64, 512, 512], P(None, 'slab', 'pencil'), may hold values from -6 to 6
- omega_ckpt: float32 [2, 3, 64, 512, 512], P(None, None, 'slab', 'pencil'), may hold values from -6 to 6
- cell_shift: int32 [2, 64, 512, 512], P(None, 'slab', 'pencil'), may hold values from -2 to 2
- move_count: int32 [2, 32, 8, 2], P(None, 'slab', 'pencil'), may hold values from 16 to 128, as said below
- move_blocks: int32 [2, 32, 8, 2, 128], P(None, 'slab', 'pencil'), may hold values from 0 to 255, as said below
Outputs:
- adjoint_out: float32 [3, 64, 512, 512], P(None, 'slab', 'pencil')
The draws below stay inside these ranges and needn't reach their ends.
Inputs may be any that keep to these rules, and one draw needn't show every extreme that they name: `move_count`: in every substep and direction some device has 128 live entries and some device 128 // 8. `move_blocks`: for each substep and device, the 256 entries are the plane-block numbers 0 to 255, each once.
All inputs are finite; a program needn't handle non-finite values.
Results may differ from the reference program's by a relative error of at most 0.00025.
Values sent between devices are 32-bit elements; how exact they have to be, the bound alone decides.
No kernel may reach another device: no remote copies, remote signals or barrier semaphores. Data moves between devices by JAX's collectives and lax.ppermute only.
A program may use at most 64 MiB of HBM per device.

```python
import math
import jax
import jax.numpy as jnp

NY = 512
NZ = 512
BL = 128
S = 2
CX = 2
SLABS = 32
PENCILS = 8
NX = 64
YP = 64
PLANE_BLOCKS = 256
MOST = 128


def draw_move_count(key, part):
    base_key, heavy_key, start_key = jax.random.split(jax.random.fold_in(key, 11), 3)
    count_shape = (S, SLABS, PENCILS, 2)
    quiet_counts = jax.random.randint(base_key, count_shape, MOST // 8, MOST // 4 + 1, dtype=jnp.int32)
    heavy_counts = jax.random.randint(heavy_key, count_shape, MOST // 2, MOST + 1, dtype=jnp.int32)
    anchor = jax.random.randint(start_key, (), 0, SLABS, dtype=jnp.int32)
    slab_index = jnp.arange(SLABS, dtype=jnp.int32)[None, :, None, None]
    pencil_index = jnp.arange(PENCILS, dtype=jnp.int32)[None, None, :, None]
    distance = (slab_index - anchor) % SLABS
    counts = jnp.where(distance < max(SLABS // 4, 1), heavy_counts, quiet_counts)
    counts = jnp.where((distance == 0) & (pencil_index == 0), MOST, counts)
    counts = jnp.where((distance == SLABS // 2) & (pencil_index == 0), MOST // 8, counts)
    return counts.astype(jnp.int32)


def draw_move_blocks(key, part):
    draw_count = S * SLABS * PENCILS
    item_keys = jax.random.split(jax.random.fold_in(key, 7), draw_count)
    orders = jax.vmap(lambda item_key: jax.random.permutation(item_key, PLANE_BLOCKS))(item_keys)
    return orders.reshape(S, SLABS, PENCILS, 2, MOST).astype(jnp.int32)


def place_ends(array, stream_key, smallest, top_value):
    longest = array.shape.index(max(array.shape))
    spots = []
    for shift in (0, 1):
        where = [jax.random.randint(jax.random.fold_in(stream_key, axis), (), 0, length) for axis, length in enumerate(array.shape)]
        where[longest] = (where[longest] + shift) % array.shape[longest]
        spots.append(tuple(where))
    return array.at[spots[0]].set(smallest).at[spots[1]].set(top_value)


def levels(own_key, extent, pieces, low, largest):
    loudness, own = 1.0, jax.random.fold_in(own_key, 6)
    for axis_at, blocks in pieces:
        steps = jnp.exp(jax.random.uniform(jax.random.fold_in(own, axis_at), (blocks,), jnp.float32, low / len(pieces), largest / len(pieces)))
        loudness = loudness * jnp.repeat(steps, extent[axis_at] // blocks).reshape([-1 if axis == axis_at else 1 for axis in range(len(extent))])
    return loudness


def gaussian(key, shape, spread, most, cuts=(), held_as=jnp.bfloat16):
    factor_of = levels(key, shape, cuts, -0.22, 0.18) if cuts else 1.0
    result = jax.random.normal(key, shape, jnp.float32) * spread * factor_of
    return jnp.minimum(jnp.maximum(result, -most), most).astype(held_as)


def setup_inputs(seed: int = 0) -> dict:
    arg_keys = jax.random.split(jax.random.key(seed), 6)
    return {
        "adjoint_vort": gaussian(arg_keys[0], (3, NX, NY, NZ), 1.0, 6.0, ((1, 32), (2, 8)), jnp.float32),
        "omega_ckpt": gaussian(arg_keys[1], (S, 3, NX, NY, NZ), 1.0, 6.0, ((2, 32), (3, 8)), jnp.float32),
        "cell_shift": place_ends(jax.random.randint(arg_keys[2], (S, NX, NY, NZ), -2, 3), jax.random.fold_in(arg_keys[2], 1), -2, 2).astype(jnp.int32),
        "move_count": draw_move_count(jax.random.fold_in(arg_keys[5], 71), 0),
        "move_blocks": draw_move_blocks(jax.random.fold_in(arg_keys[5], 71), 0),
    }


time_step = 0.25


def cross_product(first_vec, second_vec):
    return jnp.stack([
        first_vec[1] * second_vec[2] - first_vec[2] * second_vec[1],
        first_vec[2] * second_vec[0] - first_vec[0] * second_vec[2],
        first_vec[0] * second_vec[1] - first_vec[1] * second_vec[0],
    ], 0)


def remesh(adjoint, vorticity, shifts, counts, blocks):
    per_row = NZ // BL
    slab_index = jnp.arange(SLABS, dtype=jnp.int32)[:, None, None]
    pencil_index = jnp.arange(PENCILS, dtype=jnp.int32)[None, :, None]
    slot_index = jnp.arange(MOST, dtype=jnp.int32)[None, None, :]
    offsets = jnp.zeros((NX, NY, per_row), jnp.int32)
    for direction, plane_index, step_value in ((0, CX - 1, 1), (1, 0, -1)):
        chosen = blocks[:, :, direction, :]
        alive_slot = slot_index < counts[:, :, direction][:, :, None]
        plane_x = jnp.where(alive_slot, slab_index * CX + plane_index + 0 * chosen, NX).astype(jnp.int32)
        row_y = (pencil_index * YP + chosen // per_row).astype(jnp.int32)
        block_z = (chosen % per_row).astype(jnp.int32)
        offsets = offsets.at[plane_x, row_y, block_z].set(step_value, mode="drop")
    offsets = jnp.repeat(offsets, BL, axis=2)
    x_index = jnp.arange(NX, dtype=jnp.int32)[:, None, None]
    y_index = jnp.arange(NY, dtype=jnp.int32)[None, :, None]
    z_index = jnp.arange(NZ, dtype=jnp.int32)[None, None, :]
    target_x = (x_index + offsets) % NX
    target_z = (z_index + shifts) % NZ
    flat_cell = ((target_x * NY + y_index) * NZ + target_z).reshape(-1).astype(jnp.int32)
    carried = jnp.concatenate([adjoint, vorticity], 0).reshape(6, -1)
    deposit = jnp.zeros((6, NX * NY * NZ), jnp.float32).at[:, flat_cell].add(carried)
    deposit = deposit.reshape(6, NX, NY, NZ)
    return deposit[:3], deposit[3:]


def y_diff(values):
    return (jnp.roll(values, -1, 1) - jnp.roll(values, 1, 1)) * 0.5


def z_diff(values):
    return (jnp.roll(values, -1, 2) - jnp.roll(values, 1, 2)) * 0.5


def velocity(source):
    wave_y = jnp.arange(NY, dtype=jnp.int32)
    wave_z = jnp.arange(NZ, dtype=jnp.int32)
    sine_y = jnp.sin(math.pi * wave_y.astype(jnp.float32) / NY)
    sine_z = jnp.sin(math.pi * wave_z.astype(jnp.float32) / NZ)
    symbol = 4.0 * sine_y[:, None] ** 2 + 4.0 * sine_z[None, :] ** 2
    nonzero = (wave_y[:, None] + wave_z[None, :]) > 0
    factor = jnp.where(nonzero, 1.0 / jnp.where(nonzero, symbol, 1.0), 0.0)
    spectrum = jnp.fft.fft2(source, axes=(-2, -1))
    stream = jnp.real(jnp.fft.ifft2(spectrum * factor, axes=(-2, -1))).astype(jnp.float32)
    first_part = y_diff(stream[2]) - z_diff(stream[1])
    second = z_diff(stream[0])
    third_part = -y_diff(stream[0])
    return jnp.stack([first_part, second, third_part], 0)


def reference(adjoint_vort, omega_ckpt, cell_shift, move_count, move_blocks):
    adjoint = adjoint_vort
    for substep in range(S):
        remeshed, vortex = remesh(adjoint, omega_ckpt[substep], cell_shift[substep], move_count[substep], move_blocks[substep])
        velocity_field = velocity(remeshed)
        slope_x = (jnp.roll(velocity_field, -1, 1) - jnp.roll(velocity_field, 1, 1)) * 0.5
        adjoint = remeshed + time_step * (cross_product(vortex, velocity_field) + vortex[0] * slope_x)
    return adjoint
```

```python
import math

import jax
import jax.numpy as jnp
import numpy as np
from jax import lax
from jax.experimental import pallas as pl
from jax.experimental.pallas import tpu as pltpu
from jax.sharding import PartitionSpec as P

N = 512
H = 256
ROWS = 64
GROUPS = 8
BL = 128
TIME_STEP = 0.25
VMEM_LIMIT = 40 * 1024 * 1024


def lane_wave():
    m = np.arange(128)
    return np.concatenate([2 * m, np.where(m == 0, 256, 2 * m), 2 * m + 1, 2 * m + 1])


def tables():
    wave = lane_wave()
    z = np.arange(H)
    angle = 2 * np.pi * (wave[:, None] * z[None, :] % N) / N
    is_sin = np.zeros(N, bool)
    is_sin[129:256] = True
    is_sin[384:] = True
    basis = np.where(is_sin[:, None], np.sin(angle), np.cos(angle))
    forward = np.stack([basis[:H].T, basis[H:].T])
    lam = 4 * np.sin(np.pi * wave / N) ** 2
    r = 1 + lam / 2 - np.sqrt(lam + lam * lam / 4)
    norm = np.where((wave == 0) | (wave == 256), 1.0, 2.0) / N
    inverse = basis * (norm * r)[:, None]
    inverse = np.stack([inverse[:H], inverse[H:]])
    sigma = np.sin(2 * np.pi * wave / N)
    sigma[128] = 0.0
    sigma[0] = 0.0
    swap = sigma.copy()
    swap[128:256] *= -1
    swap[384:] *= -1
    rpow = r[None, :] ** (np.arange(ROWS)[:, None] + 1)

    rs = np.where(wave == 0, 0.5, r)
    rho = rs**ROWS
    wrap = 1 / (1 - rho**GROUPS)
    step = np.arange(GROUPS)
    up = np.where(step == 0, GROUPS, GROUPS - step)
    down = np.where(step == 0, GROUPS, step)
    cuu = rho[None, :] ** (up[:, None] - 1) * wrap
    cww = rho[None, :] ** (down[:, None] - 1) * wrap
    kappa = rs * (1 - rs ** (2 * ROWS)) / (1 - rs**2)
    cwu = np.zeros((GROUPS, N))
    for a in range(GROUPS):
        for b in range(GROUPS):
            cwu[(a + b) % GROUPS] += kappa * cww[a] * cuu[b]
    tri = ROWS * (ROWS + 1) // 2
    pyr = sum(tri - y * (y + 1) // 2 for y in range(ROWS))
    left, right = [], []
    row, rhs = np.zeros(17), np.zeros(24)
    row[16] = N
    rhs[:8] = 1
    left.append(row)
    right.append(rhs)
    for m in range(8):
        row, rhs = np.zeros(17), np.zeros(24)
        row[(m + 1) % 8] += 1
        row[m] -= 1
        row[16] = ROWS
        rhs[m] = 1
        left.append(row)
        right.append(rhs)
        row, rhs = np.zeros(17), np.zeros(24)
        row[8 + (m - 1) % 8] += 1
        row[8 + m] -= 1
        row[m] -= ROWS
        row[16] = tri
        rhs[8 + m] = 1
        left.append(row)
        right.append(rhs)
    row, rhs = np.zeros(17), np.zeros(24)
    row[:8] = ROWS
    row[16] = -8 * tri
    rhs[8:16] = -1
    left.append(row)
    right.append(rhs)
    row, rhs = np.zeros(17), np.zeros(24)
    row[:8] = tri
    row[8:16] = ROWS
    row[16] = -8 * pyr
    rhs[16:] = -1
    left.append(row)
    right.append(rhs)
    answer = np.linalg.lstsq(np.array(left), np.array(right), rcond=None)[0]
    cuu[:, 0] = answer[0, :8]
    cww[:, 0] = answer[8, 8:16]
    cwu[:, 0] = answer[8, :8]
    zero_u = answer[0, 8]
    zero_z = answer[8, 16]
    return {
        "forward": forward,
        "inverse": inverse,
        "swap": swap,
        "rpow": rpow,
        "r": r,
        "cuu": cuu,
        "cww": cww,
        "cwu": cwu,
        "zero_u": float(zero_u),
        "zero_z": float(zero_z),
    }


def halves(matrix):
    full = np.asarray(matrix, np.float32)
    high = full.astype(jnp.bfloat16)
    low = (full - high.astype(np.float32)).astype(jnp.bfloat16)
    return jnp.asarray(np.stack([high, low]))


def split(x):
    high = x.astype(jnp.bfloat16)
    return high, (x - high.astype(jnp.float32)).astype(jnp.bfloat16)


def dot3(x, matrix_ref, block):
    high, low = split(x)
    first = matrix_ref[0, block]
    second = matrix_ref[1, block]
    out = jnp.dot(high, first, preferred_element_type=jnp.float32)
    out = out + jnp.dot(low, first, preferred_element_type=jnp.float32)
    return out + jnp.dot(high, second, preferred_element_type=jnp.float32)


def code_kernel(count_ref, blocks_ref, shift_ref, out_ref):
    slot = lax.broadcasted_iota(jnp.int32, (1, BL), 1)
    row_id = lax.broadcasted_iota(jnp.int32, (ROWS, BL), 0)
    lane_block = lax.broadcasted_iota(jnp.int32, (N, BL), 0) // BL
    for s in range(2):
        for plane in range(2):
            direction = 1 - plane
            ids = blocks_ref[pl.ds(s * 2 + direction, 1), :]
            alive = slot < count_ref[s * 2 + direction]
            ids = jnp.where(alive, ids, -8)
            rows = jnp.where(jnp.broadcast_to(ids >> 2, (ROWS, BL)) == row_id, 1.0, 0.0)
            lanes = jnp.where(jnp.broadcast_to(ids & 3, (N, BL)) == lane_block, 1.0, 0.0)
            moved = lax.dot_general(
                rows.astype(jnp.bfloat16),
                lanes.astype(jnp.bfloat16),
                (((1,), (1,)), ((), ())),
                preferred_element_type=jnp.float32,
            )
            out_ref[s, plane] = shift_ref[s, plane] + 8 * moved.astype(jnp.int32)


def codes_of(count, blocks, shifts):
    return pl.pallas_call(
        code_kernel,
        out_shape=jax.ShapeDtypeStruct((2, 2, ROWS, N), jnp.int32),
        in_specs=[
            pl.BlockSpec(memory_space=pltpu.SMEM),
            pl.BlockSpec(memory_space=pltpu.VMEM),
            pl.BlockSpec(memory_space=pltpu.VMEM),
        ],
        out_specs=pl.BlockSpec(memory_space=pltpu.VMEM),
        compiler_params=pltpu.CompilerParams(vmem_limit_bytes=VMEM_LIMIT),
        name="codes",
    )(count, blocks, shifts)


def deposit(own, own_code, other, other_code):
    total = None
    for amount in (0, 1, 2, -1, -2):
        picked = jnp.where(own_code == amount, own, 0.0) + jnp.where(
            other_code == amount + 8, other, 0.0
        )
        if amount:
            picked = pltpu.roll(picked, amount % N, 1)
        total = picked if total is None else total + picked
    return total


def omega_kernel(own_ref, below_ref, above_ref, code_ref, cbelow_ref, cabove_ref, out_ref):
    for plane, other_ref, cother_ref in ((0, below_ref, cbelow_ref), (1, above_ref, cabove_ref)):

        @pl.loop(0, ROWS // 8)
        def _(step, plane=plane, other_ref=other_ref, cother_ref=cother_ref):
            rows = pl.ds(pl.multiple_of(step * 8, 8), 8)
            own_code = code_ref[plane, rows, :]
            other_code = cother_ref[rows, :]
            for c in range(3):
                out_ref[c, plane, rows, :] = deposit(
                    own_ref[c, plane, rows, :], own_code, other_ref[c, rows, :], other_code
                )


def omega_of(own, below, above, code, cbelow, cabove):
    return pl.pallas_call(
        omega_kernel,
        out_shape=jax.ShapeDtypeStruct((3, 2, ROWS, N), jnp.float32),
        in_specs=[pl.BlockSpec(memory_space=pltpu.VMEM)] * 6,
        out_specs=pl.BlockSpec(memory_space=pltpu.VMEM),
        compiler_params=pltpu.CompilerParams(vmem_limit_bytes=VMEM_LIMIT),
        cost_estimate=pl.CostEstimate(flops=30_000_000, bytes_accessed=6_000_000, transcendentals=0),
        name="omega",
    )(own, below, above, code, cbelow, cabove)


SUBLANE = (0, 4, 12)


def first_kernel(
    own_ref, below_ref, above_ref, code_ref, cbelow_ref, cabove_ref, forward_ref, r_ref,
    lam_ref, u_ref, ends_ref, x_ref, h_ref,
):
    for plane, other, other_ref, cother_ref in (
        (0, 0, below_ref, cbelow_ref),
        (1, 3, above_ref, cabove_ref),
    ):

        @pl.loop(0, ROWS // 8)
        def _(step, plane=plane, other=other, other_ref=other_ref, cother_ref=cother_ref):
            start = pl.multiple_of(step * 8, 8)
            rows = pl.ds(start, 8)
            own_code = code_ref[plane, rows, :]
            other_code = cother_ref[rows, :]
            for c in range(3):
                own = own_ref[c, plane, rows, :]
                far = other_ref[c, rows, :]
                here = deposit(own, own_code, far, other_code)
                there = deposit(far, other_code, own, own_code)
                lam_ref[c, plane, rows, :] = here
                for place, value in ((plane + 1, here), (other, there)):
                    base = (c * 4 + place) * ROWS
                    at = pl.ds(pl.multiple_of(base + start, 8), 8)
                    x_ref[at, :H] = value[:, :H] + value[:, H:]
                    x_ref[at, H:] = value[:, :H] - value[:, H:]

    for block in range(2):
        lanes = pl.ds(block * H, H)
        out = dot3(x_ref[:, lanes], forward_ref, block)
        for c in range(3):
            for place in range(4):
                base = (c * 4 + place) * ROWS
                for part in range(2):
                    h_ref[block * 2 + part, pl.ds(SUBLANE[c] + place, ROWS, stride=16), :] = out[
                        base : base + ROWS, part * BL : (part + 1) * BL
                    ]

    r = [jnp.broadcast_to(r_ref[:, q * BL : (q + 1) * BL], (16, BL)) for q in range(4)]
    zero = jnp.zeros((16, BL), jnp.float32)

    def ahead(y, carry):
        at = pl.ds(pl.multiple_of(y * 16, 16), 16)
        new = []
        for q in range(4):
            value = h_ref[q, at, :] + r[q] * carry[q]
            u_ref[q, at, :] = value
            new.append(value)
        return tuple(new)

    u_end = lax.fori_loop(0, ROWS, ahead, (zero,) * 4, unroll=8)

    def back(i, carry):
        y = ROWS - 1 - i
        at = pl.ds(pl.multiple_of(y * 16, 16), 16)
        new = [u_ref[q, at, :] + r[q] * carry[q] for q in range(4)]
        return (*new, carry[4] + new[0])

    w_end = lax.fori_loop(0, ROWS, back, (zero,) * 5, unroll=8)
    for q in range(4):
        lanes = pl.ds(q * BL, BL)
        ends_ref[0:8, lanes] = u_end[q][0:8]
        ends_ref[8:12, lanes] = u_end[q][12:16]
        ends_ref[12:20, lanes] = w_end[q][0:8]
        ends_ref[20:24, lanes] = w_end[q][12:16]
    lane = lax.broadcasted_iota(jnp.int32, (16, BL), 1)
    sub = lax.broadcasted_iota(jnp.int32, (16, BL), 0)
    sums = jnp.broadcast_to(w_end[4][:, 0:1], (16, BL))
    ends_ref[24:25, :] = jnp.zeros((1, N), jnp.float32)
    used = (lane == sub) & ((sub < 8) | (sub >= 12))
    ends_ref[24:25, 0:BL] = jnp.sum(jnp.where(used, sums, 0.0), axis=0, keepdims=True)


def first_of(own, below, above, code, cbelow, cabove, forward, r):
    return pl.pallas_call(
        first_kernel,
        out_shape=(
            jax.ShapeDtypeStruct((3, 2, ROWS, N), jnp.float32),
            jax.ShapeDtypeStruct((4, ROWS * 16, BL), jnp.float32),
            jax.ShapeDtypeStruct((25, N), jnp.float32),
        ),
        in_specs=[pl.BlockSpec(memory_space=pltpu.VMEM)] * 8,
        out_specs=(pl.BlockSpec(memory_space=pltpu.VMEM),) * 3,
        scratch_shapes=[
            pltpu.VMEM((12 * ROWS, N), jnp.float32),
            pltpu.VMEM((4, ROWS * 16, BL), jnp.float32),
        ],
        compiler_params=pltpu.CompilerParams(vmem_limit_bytes=VMEM_LIMIT),
        cost_estimate=pl.CostEstimate(flops=3_000_000_000, bytes_accessed=8_000_000, transcendentals=0),
        name="first",
    )(own, below, above, code, cbelow, cabove, forward, r)


def second_kernel(
    zero_u, zero_z,
    me_ref, ends_ref, u_ref, lam_ref, omega_ref, cuu_ref, cww_ref, cwu_ref, rpow_ref, r_ref,
    swap_ref, inverse_ref, out_ref, y_ref, field_ref,
):
    me = me_ref[0]
    u_in = [[jnp.zeros((8, BL), jnp.float32)] * 2 for _ in range(4)]
    w_in = [[jnp.zeros((8, BL), jnp.float32)] * 2 for _ in range(4)]
    u_sum = [jnp.zeros((8, BL), jnp.float32)] * 2
    w_sum = [jnp.zeros((8, BL), jnp.float32)] * 2
    z_row = jnp.zeros((1, BL), jnp.float32)
    for step in range(GROUPS):
        who = (me + step) & (GROUPS - 1)
        for q in range(4):
            lanes = pl.ds(q * BL, BL)
            uu = cuu_ref[step : step + 1, lanes]
            ww = cww_ref[step : step + 1, lanes]
            wu = cwu_ref[step : step + 1, lanes]
            for g in range(2):
                u = ends_ref[who, 4 * g : 4 * g + 8, lanes]
                w = ends_ref[who, 12 + 4 * g : 20 + 4 * g, lanes]
                u_in[q][g] = u_in[q][g] + uu * u
                w_in[q][g] = w_in[q][g] + (ww * w + wu * u)
                if q == 0:
                    u_sum[g] = u_sum[g] + u
                    w_sum[g] = w_sum[g] + w
        z_row = z_row + ends_ref[step, 24:25, 0:BL]
    lane = lax.broadcasted_iota(jnp.int32, (8, BL), 1)
    sub = lax.broadcasted_iota(jnp.int32, (8, BL), 0)
    first_lane = lane == 0
    mean = []
    for g in range(2):
        u_in[0][g] = u_in[0][g] + jnp.where(first_lane, zero_u * w_sum[g], 0.0)
        mean.append(jnp.where(first_lane, u_sum[g] * (1.0 / N), 0.0))
        mine = jnp.where(lane == sub + 8 * g, jnp.broadcast_to(z_row, (8, BL)), 0.0)
        z_total = jnp.broadcast_to(jnp.sum(mine, axis=1, keepdims=True), (8, BL))
        w_in[0][g] = w_in[0][g] + jnp.where(first_lane, zero_z * z_total, 0.0)

    r = [jnp.broadcast_to(r_ref[:, q * BL : (q + 1) * BL], (8, BL)) for q in range(4)]
    swap = [jnp.broadcast_to(swap_ref[:, q * BL : (q + 1) * BL], (8, BL)) for q in range(4)]
    upper = sub < 4

    def emit(y, after, here, before):
        at = pl.ds(pl.multiple_of(y * 8, 8), 8)
        at_b = pl.ds(pl.multiple_of(ROWS * 8 + y * 8, 8), 8)
        for q in range(4):
            slope0 = 0.5 * (after[2 * q] - before[2 * q])
            slope1 = 0.5 * (after[2 * q + 1] - before[2 * q + 1])
            turned = swap[q] * here[2 * (q ^ 1)]
            lanes = pl.ds(q * BL, BL)
            y_ref[at, lanes] = jnp.where(upper, here[2 * q], slope1 - turned)
            y_ref[at_b, lanes] = slope0

    def back(i, carry):
        y = ROWS - 1 - i
        after, here = carry[:8], carry[8:]
        new = []
        for q in range(4):
            power = rpow_ref[y, :, q * BL : (q + 1) * BL]
            for g in range(2):
                at = pl.ds(pl.multiple_of(y * 16 + 8 * g, 8), 8)
                value = u_ref[q, at, :] + power * u_in[q][g]
                if q == 0:
                    value = value - (y + 1).astype(jnp.float32) * mean[g]
                new.append(value + r[q] * here[2 * q + g])
        emit(y + 1, after, here, new)
        return (*here, *new)

    edge = tuple(w_in[q][g] for q in range(4) for g in range(2))
    new = []
    for q in range(4):
        power = rpow_ref[ROWS - 1, :, q * BL : (q + 1) * BL]
        for g in range(2):
            value = u_ref[q, (ROWS - 1) * 16 + 8 * g : (ROWS - 1) * 16 + 8 * g + 8, :]
            value = value + power * u_in[q][g]
            if q == 0:
                value = value - float(ROWS) * mean[g]
            new.append(value + r[q] * edge[2 * q + g])
    carry = lax.fori_loop(1, ROWS, back, (*edge, *new), unroll=3)
    after, here = carry[:8], carry[8:]
    before = [u_in[q][g] + r[q] * here[2 * q + g] for q in range(4) for g in range(2)]
    emit(jnp.int32(0), after, here, before)

    even = dot3(y_ref[:, :H], inverse_ref, 0)
    odd = dot3(y_ref[:, H:], inverse_ref, 1)
    for part in range(2):
        lanes = slice(part * BL, (part + 1) * BL)
        field_ref[part] = even[:, lanes] + odd[:, lanes]
        field_ref[2 + part] = even[:, lanes] - odd[:, lanes]

    @pl.loop(0, ROWS // 8)
    def _(step):
        start = pl.multiple_of(step * 8, 8)
        rows = pl.ds(start, 8)

        def load(base):
            parts = [
                field_ref[q, pl.ds(start * 8 + base, 8, stride=8), :]
                for q in range(4)
            ]
            return jnp.concatenate(parts, axis=1)

        g = []
        for place in range(4):
            psi = load(place)
            gx = load(4 + place)
            gz = -load(ROWS * 8 + place)
            gy = 0.5 * (pltpu.roll(psi, N - 1, 1) - pltpu.roll(psi, 1, 1))
            g.append((gx, gy, gz))
        for plane in range(2):
            here = g[plane + 1]
            w = [omega_ref[c, plane, rows, :] for c in range(3)]
            cross = (
                w[1] * here[2] - w[2] * here[1],
                w[2] * here[0] - w[0] * here[2],
                w[0] * here[1] - w[1] * here[0],
            )
            for c in range(3):
                slope = 0.5 * (g[plane + 2][c] - g[plane][c])
                out_ref[c, plane, rows, :] = lam_ref[c, plane, rows, :] + TIME_STEP * (
                    cross[c] + w[0] * slope
                )


def second_of(t, me, ends, u, lam, omega, cuu, cww, cwu, rpow, r, swap, inverse):
    def body(*refs):
        second_kernel(t["zero_u"], t["zero_z"], *refs)

    return pl.pallas_call(
        body,
        out_shape=jax.ShapeDtypeStruct((3, 2, ROWS, N), jnp.float32),
        in_specs=[pl.BlockSpec(memory_space=pltpu.SMEM)]
        + [pl.BlockSpec(memory_space=pltpu.VMEM)] * 11,
        out_specs=pl.BlockSpec(memory_space=pltpu.VMEM),
        scratch_shapes=[
            pltpu.VMEM((ROWS * 16, N), jnp.float32),
            pltpu.VMEM((4, ROWS * 16, BL), jnp.float32),
        ],
        compiler_params=pltpu.CompilerParams(vmem_limit_bytes=VMEM_LIMIT),
        cost_estimate=pl.CostEstimate(flops=4_000_000_000, bytes_accessed=8_000_000, transcendentals=0),
        name="second",
    )(me, ends, u, lam, omega, cuu, cww, cwu, rpow, r, swap, inverse)


def shifted(value, axis, by):
    count = lax.axis_size(axis)
    return lax.ppermute(value, axis, [(i, (i + by) % count) for i in range(count)])


def neighbours(lower_plane, upper_plane):
    return shifted(upper_plane, "slab", 1), shifted(lower_plane, "slab", -1)


def shards(adjoint_vort, omega_ckpt, cell_shift, move_count, move_blocks):
    t = tables()
    forward, inverse = halves(t["forward"]), halves(t["inverse"])
    f32 = {k: jnp.asarray(t[k], jnp.float32) for k in ("cuu", "cww", "cwu", "rpow")}
    r = jnp.asarray(t["r"], jnp.float32)[None]
    swap = jnp.asarray(t["swap"], jnp.float32)[None]
    me = lax.axis_index("pencil").astype(jnp.int32)[None]

    lam = adjoint_vort
    code = codes_of(move_count.reshape(4), move_blocks.reshape(4, BL), cell_shift)
    below, above = neighbours(lam[:, 0], lam[:, 1])
    far_code = [neighbours(code[s, 0], code[s, 1]) for s in range(2)]
    omega = []
    for s in range(2):
        far = neighbours(omega_ckpt[s, :, 0], omega_ckpt[s, :, 1])
        omega.append(omega_of(omega_ckpt[s], *far, code[s], *far_code[s]))
    for s in range(2):
        if s:
            below, above = neighbours(lam[:, 0], lam[:, 1])
        lam_r, u, ends = first_of(lam, below, above, code[s], *far_code[s], forward, r)
        gathered = lax.all_to_all(
            jnp.broadcast_to(ends[None], (GROUPS, 25, N)), "pencil", 0, 0, tiled=True
        )
        lam = second_of(
            t, me, gathered, u, lam_r, omega[s], f32["cuu"], f32["cww"], f32["cwu"],
            f32["rpow"][:, None], r, swap, inverse,
        )
    return lam


def solution(mesh):
    return jax.shard_map(
        shards,
        mesh=mesh,
        in_specs=(
            P(None, "slab", "pencil", None),
            P(None, None, "slab", "pencil", None),
            P(None, "slab", "pencil", None),
            P(None, "slab", "pencil", None),
            P(None, "slab", "pencil", None, None),
        ),
        out_specs=P(None, "slab", "pencil", None),
        check_vma=False,
    )
```

```python
import math

import jax
import jax.numpy as jnp
import numpy as np
from jax import lax
from jax.experimental import pallas as pl
from jax.experimental.pallas import tpu as pltpu
from jax.sharding import PartitionSpec as P

N = 512
H = 256
ROWS = 64
GROUPS = 8
BL = 128
TIME_STEP = 0.25
VMEM_LIMIT = 16 * 1024 * 1024
CUU_ROW = ROWS
CWW_ROW = CUU_ROW + GROUPS
CWU_ROW = CWW_ROW + GROUPS
R_ROW = CWU_ROW + GROUPS
SWAP_ROW = R_ROW + 1


def lane_wave():
    m = np.arange(128)
    return np.concatenate([2 * m, np.where(m == 0, 256, 2 * m), 2 * m + 1, 2 * m + 1])


def tables():
    wave = lane_wave()
    z = np.arange(H)
    angle = 2 * np.pi * (wave[:, None] * z[None, :] % N) / N
    is_sin = np.zeros(N, bool)
    is_sin[129:256] = True
    is_sin[384:] = True
    basis = np.where(is_sin[:, None], np.sin(angle), np.cos(angle))
    forward = np.stack([basis[:H].T, basis[H:].T])
    lam = 4 * np.sin(np.pi * wave / N) ** 2
    r = 1 + lam / 2 - np.sqrt(lam + lam * lam / 4)
    norm = np.where((wave == 0) | (wave == 256), 1.0, 2.0) / N
    inverse = basis * (norm * r)[:, None]
    inverse = np.stack([inverse[:H], inverse[H:]])
    sigma = np.sin(2 * np.pi * wave / N)
    sigma[128] = 0.0
    sigma[0] = 0.0
    swap = sigma.copy()
    swap[128:256] *= -1
    swap[384:] *= -1
    rpow = r[None, :] ** (np.arange(ROWS)[:, None] + 1)

    rs = np.where(wave == 0, 0.5, r)
    rho = rs**ROWS
    wrap = 1 / (1 - rho**GROUPS)
    step = np.arange(GROUPS)
    up = np.where(step == 0, GROUPS, GROUPS - step)
    down = np.where(step == 0, GROUPS, step)
    cuu = rho[None, :] ** (up[:, None] - 1) * wrap
    cww = rho[None, :] ** (down[:, None] - 1) * wrap
    kappa = rs * (1 - rs ** (2 * ROWS)) / (1 - rs**2)
    cwu = np.zeros((GROUPS, N))
    for a in range(GROUPS):
        for b in range(GROUPS):
            cwu[(a + b) % GROUPS] += kappa * cww[a] * cuu[b]
    tri = ROWS * (ROWS + 1) // 2
    pyr = sum(tri - y * (y + 1) // 2 for y in range(ROWS))
    left, right = [], []
    row, rhs = np.zeros(17), np.zeros(24)
    row[16] = N
    rhs[:8] = 1
    left.append(row)
    right.append(rhs)
    for m in range(8):
        row, rhs = np.zeros(17), np.zeros(24)
        row[(m + 1) % 8] += 1
        row[m] -= 1
        row[16] = ROWS
        rhs[m] = 1
        left.append(row)
        right.append(rhs)
        row, rhs = np.zeros(17), np.zeros(24)
        row[8 + (m - 1) % 8] += 1
        row[8 + m] -= 1
        row[m] -= ROWS
        row[16] = tri
        rhs[8 + m] = 1
        left.append(row)
        right.append(rhs)
    row, rhs = np.zeros(17), np.zeros(24)
    row[:8] = ROWS
    row[16] = -8 * tri
    rhs[8:16] = -1
    left.append(row)
    right.append(rhs)
    row, rhs = np.zeros(17), np.zeros(24)
    row[:8] = tri
    row[8:16] = ROWS
    row[16] = -8 * pyr
    rhs[16:] = -1
    left.append(row)
    right.append(rhs)
    answer = np.linalg.lstsq(np.array(left), np.array(right), rcond=None)[0]
    cuu[:, 0] = answer[0, :8]
    cww[:, 0] = answer[8, 8:16]
    cwu[:, 0] = answer[8, :8]
    zero_u = answer[0, 8]
    zero_z = answer[8, 16]
    return {
        "forward": forward,
        "inverse": inverse,
        "swap": swap,
        "rpow": rpow,
        "r": r,
        "cuu": cuu,
        "cww": cww,
        "cwu": cwu,
        "zero_u": float(zero_u),
        "zero_z": float(zero_z),
    }


def halves(matrix):
    full = np.asarray(matrix, np.float32)
    high = full.astype(jnp.bfloat16)
    low = (full - high.astype(np.float32)).astype(jnp.bfloat16)
    return jnp.asarray(np.stack([high, low]))


def split(x):
    high = x.astype(jnp.bfloat16)
    return high, (x - high.astype(jnp.float32)).astype(jnp.bfloat16)


def dot3(x, matrix_ref, block):
    high, low = split(x)
    first = matrix_ref[0, block]
    second = matrix_ref[1, block]
    out = jnp.dot(high, first, preferred_element_type=jnp.float32)
    out = out + jnp.dot(low, first, preferred_element_type=jnp.float32)
    return out + jnp.dot(high, second, preferred_element_type=jnp.float32)


def live_ids(count_ref, blocks_ref, s, direction):
    slot = lax.broadcasted_iota(jnp.int32, (1, BL), 1)
    ids = blocks_ref[s, 0, 0, direction : direction + 1, :]
    return jnp.where(slot < count_ref[s, 0, 0, direction], ids, -8)


def code_kernel(count_ref, blocks_ref, shift_ref, *out_refs):
    row_id = lax.broadcasted_iota(jnp.int32, (ROWS, BL), 0)
    lane_block = lax.broadcasted_iota(jnp.int32, (N, BL), 0) // BL
    for s in range(2):
        for plane in range(2):
            ids = live_ids(count_ref, blocks_ref, s, 1 - plane)
            rows = jnp.where(jnp.broadcast_to(ids >> 2, (ROWS, BL)) == row_id, 1.0, 0.0)
            lanes = jnp.where(jnp.broadcast_to(ids & 3, (N, BL)) == lane_block, 1.0, 0.0)
            moved = lax.dot_general(
                rows.astype(jnp.bfloat16),
                lanes.astype(jnp.bfloat16),
                (((1,), (1,)), ((), ())),
                preferred_element_type=jnp.float32,
            )
            out_refs[2 * s + plane][...] = shift_ref[s, plane] + 8 * moved.astype(jnp.int32)


def codes_of(count, blocks, shifts):
    return pl.pallas_call(
        code_kernel,
        out_shape=(jax.ShapeDtypeStruct((ROWS, N), jnp.int32),) * 4,
        in_specs=[
            pl.BlockSpec(memory_space=pltpu.SMEM),
            pl.BlockSpec(memory_space=pltpu.VMEM),
            pl.BlockSpec(memory_space=pltpu.VMEM),
        ],
        out_specs=(pl.BlockSpec(memory_space=pltpu.VMEM),) * 4,
        compiler_params=pltpu.CompilerParams(vmem_limit_bytes=VMEM_LIMIT),
        cost_estimate=pl.CostEstimate(flops=40_000_000, bytes_accessed=1_000_000, transcendentals=0),
        name="codes",
    )(count, blocks, shifts)


def parts_of(x):
    high = x.astype(jnp.bfloat16)
    rest = x - high.astype(jnp.float32)
    middle = rest.astype(jnp.bfloat16)
    return high, middle, (rest - middle.astype(jnp.float32)).astype(jnp.bfloat16)


def chosen_rows(ids, q):
    row_id = lax.broadcasted_iota(jnp.int32, (ROWS, BL), 0)
    wide = jnp.broadcast_to(ids, (ROWS, BL))
    hit = ((wide >> 2) == row_id) & ((wide & 3) == q)
    return jnp.where(hit, 1.0, 0.0).astype(jnp.bfloat16)


def pack_kernel(count_ref, blocks_ref, omega_ref, *out_refs):
    for s in range(2):
        for plane in range(2):
            ids = live_ids(count_ref, blocks_ref, s, 1 - plane)
            out_ref = out_refs[2 * s + plane]
            total = jnp.zeros((BL, 3 * BL), jnp.float32)
            for q in range(4):
                chosen = chosen_rows(ids, q)
                lanes = slice(q * BL, (q + 1) * BL)
                x = jnp.concatenate([omega_ref[s, c, plane, :, lanes] for c in range(3)], axis=1)
                for part in parts_of(x):
                    total = total + lax.dot_general(
                        chosen, part, (((0,), (0,)), ((), ())), preferred_element_type=jnp.float32
                    )
            out_ref[0:BL, :] = total
            out_ref[BL : BL + 8, :] = jnp.zeros((8, 3 * BL), jnp.float32)
            out_ref[BL : BL + 1, 0:BL] = ids.astype(jnp.float32)


def packed_of(count, blocks, omega):
    return pl.pallas_call(
        pack_kernel,
        out_shape=(jax.ShapeDtypeStruct((BL + 8, 3 * BL), jnp.float32),) * 4,
        in_specs=[
            pl.BlockSpec(memory_space=pltpu.SMEM),
            pl.BlockSpec(memory_space=pltpu.VMEM),
            pl.BlockSpec(memory_space=pltpu.VMEM),
        ],
        out_specs=(pl.BlockSpec(memory_space=pltpu.VMEM),) * 4,
        compiler_params=pltpu.CompilerParams(vmem_limit_bytes=VMEM_LIMIT),
        cost_estimate=pl.CostEstimate(flops=300_000_000, bytes_accessed=3_000_000, transcendentals=0),
        name="pack",
    )(count, blocks, omega)


def deposit(own, own_code, other, other_code):
    total = None
    for amount in (0, 1, 2, -1, -2):
        picked = jnp.where(own_code == amount, own, 0.0) + jnp.where(
            other_code == amount + 8, other, 0.0
        )
        if amount:
            picked = pltpu.roll(picked, amount % N, 1)
        total = picked if total is None else total + picked
    return total


def omega_kernel(
    s, own_ref, below_ref, above_ref, code0_ref, code1_ref, cbelow_ref, cabove_ref, out_ref, far_ref
):
    for plane, other_ref, code_ref, cother_ref in (
        (0, below_ref, code0_ref, cbelow_ref),
        (1, above_ref, code1_ref, cabove_ref),
    ):
        ids = other_ref[BL : BL + 1, 0:BL].astype(jnp.int32)
        parts = parts_of(other_ref[0:BL, :])
        for q in range(4):
            chosen = chosen_rows(ids, q)
            total = None
            for part in parts:
                term = jnp.dot(chosen, part, preferred_element_type=jnp.float32)
                total = term if total is None else total + term
            for c in range(3):
                far_ref[c, :, q * BL : (q + 1) * BL] = total[:, c * BL : (c + 1) * BL]

        @pl.loop(0, ROWS // 8)
        def _(step, plane=plane, code_ref=code_ref, cother_ref=cother_ref):
            rows = pl.ds(pl.multiple_of(step * 8, 8), 8)
            own_code = code_ref[rows, :]
            other_code = cother_ref[rows, :]
            for c in range(3):
                out_ref[c, plane, rows, :] = deposit(
                    own_ref[s, c, plane, rows, :], own_code, far_ref[c, rows, :], other_code
                )


def omega_of(s, *args):
    def body(*refs):
        omega_kernel(s, *refs)

    return pl.pallas_call(
        body,
        out_shape=jax.ShapeDtypeStruct((3, 2, ROWS, N), jnp.float32),
        in_specs=[pl.BlockSpec(memory_space=pltpu.VMEM)] * 7,
        out_specs=pl.BlockSpec(memory_space=pltpu.VMEM),
        scratch_shapes=[pltpu.VMEM((3, ROWS, N), jnp.float32)],
        compiler_params=pltpu.CompilerParams(vmem_limit_bytes=VMEM_LIMIT),
        cost_estimate=pl.CostEstimate(flops=300_000_000, bytes_accessed=6_000_000, transcendentals=0),
        name="omega",
    )(*args)


SUBLANE = (0, 4, 12)


def first_kernel(
    own0_ref, own1_ref, below_ref, above_ref, code0_ref, code1_ref, cbelow_ref, cabove_ref,
    forward_ref, table_ref, lam_ref, u_ref, ends_ref, x_ref, h_ref,
):
    for plane, other, own_ref, other_ref, code_ref, cother_ref in (
        (0, 0, own0_ref, below_ref, code0_ref, cbelow_ref),
        (1, 3, own1_ref, above_ref, code1_ref, cabove_ref),
    ):

        @pl.loop(0, ROWS // 8)
        def _(
            step, plane=plane, other=other, own_ref=own_ref, other_ref=other_ref,
            code_ref=code_ref, cother_ref=cother_ref,
        ):
            start = pl.multiple_of(step * 8, 8)
            rows = pl.ds(start, 8)
            own_code = code_ref[rows, :]
            other_code = cother_ref[rows, :]
            for c in range(3):
                own = own_ref[c, rows, :]
                far = other_ref[c, rows, :]
                here = deposit(own, own_code, far, other_code)
                there = deposit(far, other_code, own, own_code)
                lam_ref[c, plane, rows, :] = here
                for place, value in ((plane + 1, here), (other, there)):
                    base = (c * 4 + place) * ROWS
                    at = pl.ds(pl.multiple_of(base + start, 8), 8)
                    x_ref[at, :H] = value[:, :H] + value[:, H:]
                    x_ref[at, H:] = value[:, :H] - value[:, H:]

    for block in range(2):
        lanes = pl.ds(block * H, H)
        out = dot3(x_ref[:, lanes], forward_ref, block)
        for c in range(3):
            for place in range(4):
                base = (c * 4 + place) * ROWS
                for part in range(2):
                    h_ref[block * 2 + part, pl.ds(SUBLANE[c] + place, ROWS, stride=16), :] = out[
                        base : base + ROWS, part * BL : (part + 1) * BL
                    ]

    r = [jnp.broadcast_to(table_ref[R_ROW, :, q * BL : (q + 1) * BL], (16, BL)) for q in range(4)]
    zero = jnp.zeros((16, BL), jnp.float32)

    def ahead(y, carry):
        at = pl.ds(pl.multiple_of(y * 16, 16), 16)
        new = []
        for q in range(4):
            value = h_ref[q, at, :] + r[q] * carry[q]
            u_ref[q, at, :] = value
            new.append(value)
        return tuple(new)

    u_end = lax.fori_loop(0, ROWS, ahead, (zero,) * 4, unroll=8)

    def back(i, carry):
        y = ROWS - 1 - i
        at = pl.ds(pl.multiple_of(y * 16, 16), 16)
        new = [u_ref[q, at, :] + r[q] * carry[q] for q in range(4)]
        return (*new, carry[4] + new[0])

    w_end = lax.fori_loop(0, ROWS, back, (zero,) * 5, unroll=8)
    for q in range(4):
        lanes = pl.ds(q * BL, BL)
        ends_ref[0:8, lanes] = u_end[q][0:8]
        ends_ref[8:12, lanes] = u_end[q][12:16]
        ends_ref[12:20, lanes] = w_end[q][0:8]
        ends_ref[20:24, lanes] = w_end[q][12:16]
    lane = lax.broadcasted_iota(jnp.int32, (16, BL), 1)
    sub = lax.broadcasted_iota(jnp.int32, (16, BL), 0)
    sums = jnp.broadcast_to(w_end[4][:, 0:1], (16, BL))
    ends_ref[24:25, :] = jnp.zeros((1, N), jnp.float32)
    used = (lane == sub) & ((sub < 8) | (sub >= 12))
    ends_ref[24:25, 0:BL] = jnp.sum(jnp.where(used, sums, 0.0), axis=0, keepdims=True)


def first_of(*args):
    return pl.pallas_call(
        first_kernel,
        out_shape=(
            jax.ShapeDtypeStruct((3, 2, ROWS, N), jnp.float32),
            jax.ShapeDtypeStruct((4, ROWS * 16, BL), jnp.float32),
            jax.ShapeDtypeStruct((25, N), jnp.float32),
        ),
        in_specs=[pl.BlockSpec(memory_space=pltpu.VMEM)] * 10,
        out_specs=(pl.BlockSpec(memory_space=pltpu.VMEM),) * 3,
        scratch_shapes=[
            pltpu.VMEM((12 * ROWS, N), jnp.float32),
            pltpu.VMEM((4, ROWS * 16, BL), jnp.float32),
        ],
        compiler_params=pltpu.CompilerParams(vmem_limit_bytes=VMEM_LIMIT),
        cost_estimate=pl.CostEstimate(flops=3_000_000_000, bytes_accessed=8_000_000, transcendentals=0),
        name="first",
    )(*args)


def second_kernel(
    zero_u, zero_z, last, me_ref, *refs
):
    ends_refs = refs[:GROUPS]
    u_ref, lam_ref, omega_ref, table_ref, inverse_ref = refs[GROUPS : GROUPS + 5]
    out_refs = refs[GROUPS + 5 : -2]
    y_ref, field_ref = refs[-2:]
    me = me_ref[0]
    u_in = [[jnp.zeros((8, BL), jnp.float32)] * 2 for _ in range(4)]
    w_in = [[jnp.zeros((8, BL), jnp.float32)] * 2 for _ in range(4)]
    u_sum = [jnp.zeros((8, BL), jnp.float32)] * 2
    w_sum = [jnp.zeros((8, BL), jnp.float32)] * 2
    z_row = jnp.zeros((1, BL), jnp.float32)
    for step in range(GROUPS):
        ends_ref = ends_refs[step]
        who = (me ^ step) - me & (GROUPS - 1)
        for q in range(4):
            lanes = pl.ds(q * BL, BL)
            uu = table_ref[CUU_ROW + who, :, lanes]
            ww = table_ref[CWW_ROW + who, :, lanes]
            wu = table_ref[CWU_ROW + who, :, lanes]
            for g in range(2):
                u = ends_ref[4 * g : 4 * g + 8, lanes]
                w = ends_ref[12 + 4 * g : 20 + 4 * g, lanes]
                u_in[q][g] = u_in[q][g] + uu * u
                w_in[q][g] = w_in[q][g] + (ww * w + wu * u)
                if q == 0:
                    u_sum[g] = u_sum[g] + u
                    w_sum[g] = w_sum[g] + w
        z_row = z_row + ends_ref[24:25, 0:BL]
    lane = lax.broadcasted_iota(jnp.int32, (8, BL), 1)
    sub = lax.broadcasted_iota(jnp.int32, (8, BL), 0)
    first_lane = lane == 0
    mean = []
    for g in range(2):
        u_in[0][g] = u_in[0][g] + jnp.where(first_lane, zero_u * w_sum[g], 0.0)
        mean.append(jnp.where(first_lane, u_sum[g] * (1.0 / N), 0.0))
        mine = jnp.where(lane == sub + 8 * g, jnp.broadcast_to(z_row, (8, BL)), 0.0)
        z_total = jnp.broadcast_to(jnp.sum(mine, axis=1, keepdims=True), (8, BL))
        w_in[0][g] = w_in[0][g] + jnp.where(first_lane, zero_z * z_total, 0.0)

    r = [jnp.broadcast_to(table_ref[R_ROW, :, q * BL : (q + 1) * BL], (8, BL)) for q in range(4)]
    swap = [
        jnp.broadcast_to(table_ref[SWAP_ROW, :, q * BL : (q + 1) * BL], (8, BL)) for q in range(4)
    ]
    upper = sub < 4

    def emit(y, after, here, before):
        at = pl.ds(pl.multiple_of(y * 8, 8), 8)
        at_b = pl.ds(pl.multiple_of(ROWS * 8 + y * 8, 8), 8)
        for q in range(4):
            slope0 = 0.5 * (after[2 * q] - before[2 * q])
            slope1 = 0.5 * (after[2 * q + 1] - before[2 * q + 1])
            turned = swap[q] * here[2 * (q ^ 1)]
            lanes = pl.ds(q * BL, BL)
            y_ref[at, lanes] = jnp.where(upper, here[2 * q], slope1 - turned)
            y_ref[at_b, lanes] = slope0

    def back(i, carry):
        y = ROWS - 1 - i
        after, here = carry[:8], carry[8:]
        new = []
        for q in range(4):
            power = table_ref[y, :, q * BL : (q + 1) * BL]
            for g in range(2):
                at = pl.ds(pl.multiple_of(y * 16 + 8 * g, 8), 8)
                value = u_ref[q, at, :] + power * u_in[q][g]
                if q == 0:
                    value = value - (y + 1).astype(jnp.float32) * mean[g]
                new.append(value + r[q] * here[2 * q + g])
        emit(y + 1, after, here, new)
        return (*here, *new)

    edge = tuple(w_in[q][g] for q in range(4) for g in range(2))
    new = []
    for q in range(4):
        power = table_ref[ROWS - 1, :, q * BL : (q + 1) * BL]
        for g in range(2):
            value = u_ref[q, (ROWS - 1) * 16 + 8 * g : (ROWS - 1) * 16 + 8 * g + 8, :]
            value = value + power * u_in[q][g]
            if q == 0:
                value = value - float(ROWS) * mean[g]
            new.append(value + r[q] * edge[2 * q + g])
    carry = lax.fori_loop(1, ROWS, back, (*edge, *new), unroll=3)
    after, here = carry[:8], carry[8:]
    before = [u_in[q][g] + r[q] * here[2 * q + g] for q in range(4) for g in range(2)]
    emit(jnp.int32(0), after, here, before)

    even = dot3(y_ref[:, :H], inverse_ref, 0)
    odd = dot3(y_ref[:, H:], inverse_ref, 1)
    for part in range(2):
        lanes = slice(part * BL, (part + 1) * BL)
        field_ref[part] = even[:, lanes] + odd[:, lanes]
        field_ref[2 + part] = even[:, lanes] - odd[:, lanes]

    @pl.loop(0, ROWS // 8)
    def _(step):
        start = pl.multiple_of(step * 8, 8)
        rows = pl.ds(start, 8)

        def load(base):
            parts = [
                field_ref[q, pl.ds(start * 8 + base, 8, stride=8), :]
                for q in range(4)
            ]
            return jnp.concatenate(parts, axis=1)

        g = []
        for place in range(4):
            psi = load(place)
            gx = load(4 + place)
            gz = -load(ROWS * 8 + place)
            gy = 0.5 * (pltpu.roll(psi, N - 1, 1) - pltpu.roll(psi, 1, 1))
            g.append((gx, gy, gz))
        for plane in range(2):
            here = g[plane + 1]
            w = [omega_ref[c, plane, rows, :] for c in range(3)]
            cross = (
                w[1] * here[2] - w[2] * here[1],
                w[2] * here[0] - w[0] * here[2],
                w[0] * here[1] - w[1] * here[0],
            )
            for c in range(3):
                slope = 0.5 * (g[plane + 2][c] - g[plane][c])
                new = lam_ref[c, plane, rows, :] + TIME_STEP * (cross[c] + w[0] * slope)
                if last:
                    out_refs[0][c, plane, rows, :] = new
                else:
                    out_refs[plane][c, rows, :] = new


def second_of(t, last, *args):
    def body(*refs):
        second_kernel(t["zero_u"], t["zero_z"], last, *refs)

    if last:
        shapes = (jax.ShapeDtypeStruct((3, 2, ROWS, N), jnp.float32),)
    else:
        shapes = (jax.ShapeDtypeStruct((3, ROWS, N), jnp.float32),) * 2
    return pl.pallas_call(
        body,
        out_shape=shapes,
        in_specs=[pl.BlockSpec(memory_space=pltpu.SMEM)]
        + [pl.BlockSpec(memory_space=pltpu.VMEM)] * (GROUPS + 5),
        out_specs=(pl.BlockSpec(memory_space=pltpu.VMEM),) * len(shapes),
        scratch_shapes=[
            pltpu.VMEM((ROWS * 16, N), jnp.float32),
            pltpu.VMEM((4, ROWS * 16, BL), jnp.float32),
        ],
        compiler_params=pltpu.CompilerParams(vmem_limit_bytes=VMEM_LIMIT),
        cost_estimate=pl.CostEstimate(flops=4_000_000_000, bytes_accessed=8_000_000, transcendentals=0),
        name="second",
    )(*args)


def shifted(value, axis, by):
    count = lax.axis_size(axis)
    return lax.ppermute(value, axis, [(i, (i + by) % count) for i in range(count)])


def neighbours(lower_plane, upper_plane):
    return shifted(upper_plane, "slab", 1), shifted(lower_plane, "slab", -1)


def crossed(value, mask):
    return lax.ppermute(value, "pencil", [(i, i ^ mask) for i in range(GROUPS)])


def gathered(ends):
    far = [ends] + [crossed(ends, 2 * d) for d in (1, 2, 3)]
    out = []
    for value in far:
        out += [value, crossed(value, 1)]
    return out


def shards(adjoint_vort, omega_ckpt, cell_shift, move_count, move_blocks):
    t = tables()
    forward, inverse = halves(t["forward"]), halves(t["inverse"])
    rows = [t["rpow"], t["cuu"], t["cww"], t["cwu"], t["r"][None], t["swap"][None]]
    table = jnp.asarray(np.concatenate(rows)[:, None], jnp.float32)
    me = lax.axis_index("pencil").astype(jnp.int32)[None]

    lam0, lam1 = adjoint_vort[:, 0], adjoint_vort[:, 1]
    below, above = neighbours(lam0, lam1)
    code = codes_of(move_count, move_blocks, cell_shift)
    far_code = [neighbours(code[2 * s], code[2 * s + 1]) for s in range(2)]
    packed = packed_of(move_count, move_blocks, omega_ckpt)
    far_omega = [neighbours(packed[2 * s], packed[2 * s + 1]) for s in range(2)]
    for s in range(2):
        if s:
            below, above = neighbours(lam0, lam1)
        codes = (code[2 * s], code[2 * s + 1], *far_code[s])
        omega = omega_of(s, omega_ckpt, *far_omega[s], *codes)
        lam_r, u, ends = first_of(lam0, lam1, below, above, *codes, forward, table)
        out = second_of(t, s == 1, me, *gathered(ends), u, lam_r, omega, table, inverse)
        if s == 0:
            lam0, lam1 = out
    return out[0]


def solution(mesh):
    return jax.shard_map(
        shards,
        mesh=mesh,
        in_specs=(
            P(None, "slab", "pencil", None),
            P(None, None, "slab", "pencil", None),
            P(None, "slab", "pencil", None),
            P(None, "slab", "pencil", None),
            P(None, "slab", "pencil", None, None),
        ),
        out_specs=P(None, "slab", "pencil", None),
        check_vma=False,
    )
```

```python
import math

import jax
import jax.numpy as jnp
import numpy as np
from jax import lax
from jax.experimental import pallas as pl
from jax.experimental.pallas import tpu as pltpu
from jax.sharding import PartitionSpec as P

N = 512
H = 256
ROWS = 64
GROUPS = 8
BL = 128
TIME_STEP = 0.25
VMEM_LIMIT = 16 * 1024 * 1024
CUU_ROW = ROWS
CWW_ROW = CUU_ROW + GROUPS
CWU_ROW = CWW_ROW + GROUPS
R_ROW = CWU_ROW + GROUPS
SWAP_ROW = R_ROW + 1


def lane_wave():
    m = np.arange(128)
    return np.concatenate([2 * m, np.where(m == 0, 256, 2 * m), 2 * m + 1, 2 * m + 1])


def tables():
    wave = lane_wave()
    z = np.arange(H)
    angle = 2 * np.pi * (wave[:, None] * z[None, :] % N) / N
    is_sin = np.zeros(N, bool)
    is_sin[129:256] = True
    is_sin[384:] = True
    basis = np.where(is_sin[:, None], np.sin(angle), np.cos(angle))
    forward = np.stack([basis[:H].T, basis[H:].T])
    lam = 4 * np.sin(np.pi * wave / N) ** 2
    r = 1 + lam / 2 - np.sqrt(lam + lam * lam / 4)
    norm = np.where((wave == 0) | (wave == 256), 1.0, 2.0) / N
    inverse = basis * (norm * r)[:, None]
    inverse = np.stack([inverse[:H], inverse[H:]])
    sigma = np.sin(2 * np.pi * wave / N)
    sigma[128] = 0.0
    sigma[0] = 0.0
    swap = sigma.copy()
    swap[128:256] *= -1
    swap[384:] *= -1
    rpow = r[None, :] ** (np.arange(ROWS)[:, None] + 1)

    rs = np.where(wave == 0, 0.5, r)
    rho = rs**ROWS
    wrap = 1 / (1 - rho**GROUPS)
    step = np.arange(GROUPS)
    up = np.where(step == 0, GROUPS, GROUPS - step)
    down = np.where(step == 0, GROUPS, step)
    cuu = rho[None, :] ** (up[:, None] - 1) * wrap
    cww = rho[None, :] ** (down[:, None] - 1) * wrap
    kappa = rs * (1 - rs ** (2 * ROWS)) / (1 - rs**2)
    cwu = np.zeros((GROUPS, N))
    for a in range(GROUPS):
        for b in range(GROUPS):
            cwu[(a + b) % GROUPS] += kappa * cww[a] * cuu[b]
    tri = ROWS * (ROWS + 1) // 2
    pyr = sum(tri - y * (y + 1) // 2 for y in range(ROWS))
    left, right = [], []
    row, rhs = np.zeros(17), np.zeros(24)
    row[16] = N
    rhs[:8] = 1
    left.append(row)
    right.append(rhs)
    for m in range(8):
        row, rhs = np.zeros(17), np.zeros(24)
        row[(m + 1) % 8] += 1
        row[m] -= 1
        row[16] = ROWS
        rhs[m] = 1
        left.append(row)
        right.append(rhs)
        row, rhs = np.zeros(17), np.zeros(24)
        row[8 + (m - 1) % 8] += 1
        row[8 + m] -= 1
        row[m] -= ROWS
        row[16] = tri
        rhs[8 + m] = 1
        left.append(row)
        right.append(rhs)
    row, rhs = np.zeros(17), np.zeros(24)
    row[:8] = ROWS
    row[16] = -8 * tri
    rhs[8:16] = -1
    left.append(row)
    right.append(rhs)
    row, rhs = np.zeros(17), np.zeros(24)
    row[:8] = tri
    row[8:16] = ROWS
    row[16] = -8 * pyr
    rhs[16:] = -1
    left.append(row)
    right.append(rhs)
    answer = np.linalg.lstsq(np.array(left), np.array(right), rcond=None)[0]
    cuu[:, 0] = answer[0, :8]
    cww[:, 0] = answer[8, 8:16]
    cwu[:, 0] = answer[8, :8]
    zero_u = answer[0, 8]
    zero_z = answer[8, 16]
    return {
        "forward": forward,
        "inverse": inverse,
        "swap": swap,
        "rpow": rpow,
        "r": r,
        "cuu": cuu,
        "cww": cww,
        "cwu": cwu,
        "zero_u": float(zero_u),
        "zero_z": float(zero_z),
    }


def halves(matrix):
    full = np.asarray(matrix, np.float32)
    high = full.astype(jnp.bfloat16)
    low = (full - high.astype(np.float32)).astype(jnp.bfloat16)
    return jnp.asarray(np.stack([high, low]))


def split(x):
    high = x.astype(jnp.bfloat16)
    return high, (x - high.astype(jnp.float32)).astype(jnp.bfloat16)


def dot3(x, matrix_ref, block):
    high, low = split(x)
    first = matrix_ref[0, block]
    second = matrix_ref[1, block]
    out = jnp.dot(high, first, preferred_element_type=jnp.float32)
    out = out + jnp.dot(low, first, preferred_element_type=jnp.float32)
    return out + jnp.dot(high, second, preferred_element_type=jnp.float32)


def live_ids(count_ref, blocks_ref, s, direction):
    slot = lax.broadcasted_iota(jnp.int32, (1, BL), 1)
    ids = blocks_ref[s, 0, 0, direction : direction + 1, :]
    return jnp.where(slot < count_ref[s, 0, 0, direction], ids, -8)


def moved_of(ids):
    row_id = lax.broadcasted_iota(jnp.int32, (ROWS, BL), 0)
    lane_block = lax.broadcasted_iota(jnp.int32, (N, BL), 0) // BL
    rows = jnp.where(jnp.broadcast_to(ids >> 2, (ROWS, BL)) == row_id, 1.0, 0.0)
    lanes = jnp.where(jnp.broadcast_to(ids & 3, (N, BL)) == lane_block, 1.0, 0.0)
    return lax.dot_general(
        rows.astype(jnp.bfloat16),
        lanes.astype(jnp.bfloat16),
        (((1,), (1,)), ((), ())),
        preferred_element_type=jnp.float32,
    )


def early_kernel(count_hbm, blocks_hbm, shift_hbm, lam_hbm, low_ref, high_ref, count_ref, blocks_ref, shift_ref, sem):
    copies = [
        pltpu.make_async_copy(count_hbm, count_ref, sem.at[0]),
        pltpu.make_async_copy(blocks_hbm.at[0], blocks_ref, sem.at[1]),
        pltpu.make_async_copy(shift_hbm.at[0], shift_ref, sem.at[2]),
        pltpu.make_async_copy(lam_hbm.at[:, 0], low_ref.at[pl.ds(0, 3)], sem.at[3]),
        pltpu.make_async_copy(lam_hbm.at[:, 1], high_ref.at[pl.ds(0, 3)], sem.at[4]),
    ]
    for copy in copies:
        copy.start()
    for copy in copies[:3]:
        copy.wait()
    slot = lax.broadcasted_iota(jnp.int32, (1, BL), 1)
    for plane, out_ref in ((0, low_ref), (1, high_ref)):
        direction = 1 - plane
        ids = blocks_ref[0, 0, direction : direction + 1, :]
        ids = jnp.where(slot < count_ref[0, 0, 0, direction], ids, -8)
        out_ref[3] = shift_ref[plane].astype(jnp.float32) + 8.0 * moved_of(ids)
    for copy in copies[3:]:
        copy.wait()


def early_of(count, blocks, shifts, lam):
    return pl.pallas_call(
        early_kernel,
        out_shape=(jax.ShapeDtypeStruct((4, ROWS, N), jnp.float32),) * 2,
        in_specs=[pl.BlockSpec(memory_space=pltpu.HBM)] * 4,
        out_specs=(pl.BlockSpec(memory_space=pltpu.VMEM),) * 2,
        scratch_shapes=[
            pltpu.SMEM(count.shape, jnp.int32),
            pltpu.VMEM(blocks.shape[1:], jnp.int32),
            pltpu.VMEM((2, ROWS, N), jnp.int32),
            pltpu.SemaphoreType.DMA((5,)),
        ],
        compiler_params=pltpu.CompilerParams(vmem_limit_bytes=VMEM_LIMIT),
        cost_estimate=pl.CostEstimate(flops=40_000_000, bytes_accessed=1_000_000, transcendentals=0),
        name="early",
    )(count, blocks, shifts, lam)


def parts_of(x):
    high = x.astype(jnp.bfloat16)
    rest = x - high.astype(jnp.float32)
    middle = rest.astype(jnp.bfloat16)
    return high, middle, (rest - middle.astype(jnp.float32)).astype(jnp.bfloat16)


def chosen_rows(ids, q):
    row_id = lax.broadcasted_iota(jnp.int32, (ROWS, BL), 0)
    wide = jnp.broadcast_to(ids, (ROWS, BL))
    hit = ((wide >> 2) == row_id) & ((wide & 3) == q)
    return jnp.where(hit, 1.0, 0.0).astype(jnp.bfloat16)


def pack_kernel(count_ref, blocks_ref, shift_ref, omega_ref, *out_refs):
    for plane, out_ref in enumerate(out_refs):
        out_ref[2 * BL :, :] = jnp.zeros((8, N), jnp.float32)
        for s in range(2):
            ids = live_ids(count_ref, blocks_ref, s, 1 - plane)
            out_ref[2 * BL + s : 2 * BL + s + 1, 0:BL] = ids.astype(jnp.float32)
            total = jnp.zeros((BL, 3 * BL), jnp.float32)
            for q in range(4):
                chosen = chosen_rows(ids, q)
                lanes = slice(q * BL, (q + 1) * BL)
                x = jnp.concatenate([omega_ref[s, c, plane, :, lanes] for c in range(3)], axis=1)
                for part in parts_of(x):
                    total = total + lax.dot_general(
                        chosen, part, (((0,), (0,)), ((), ())), preferred_element_type=jnp.float32
                    )
            out_ref[s * BL : (s + 1) * BL, 0 : 3 * BL] = total
        code = shift_ref[1, plane].astype(jnp.float32) + 8.0 * moved_of(ids)
        for q in range(4):
            out_ref[q * ROWS : (q + 1) * ROWS, 3 * BL :] = code[:, q * BL : (q + 1) * BL]


def packed_of(count, blocks, shifts, omega):
    return pl.pallas_call(
        pack_kernel,
        out_shape=(jax.ShapeDtypeStruct((2 * BL + 8, N), jnp.float32),) * 2,
        in_specs=[
            pl.BlockSpec(memory_space=pltpu.SMEM),
            pl.BlockSpec(memory_space=pltpu.VMEM),
            pl.BlockSpec(memory_space=pltpu.VMEM),
            pl.BlockSpec(memory_space=pltpu.VMEM),
        ],
        out_specs=(pl.BlockSpec(memory_space=pltpu.VMEM),) * 2,
        compiler_params=pltpu.CompilerParams(vmem_limit_bytes=VMEM_LIMIT),
        cost_estimate=pl.CostEstimate(flops=300_000_000, bytes_accessed=3_000_000, transcendentals=0),
        name="pack",
    )(count, blocks, shifts, omega)


def code_rows(s, early_ref, packed_ref, start):
    if s == 0:
        return early_ref[3, pl.ds(start, 8), :]
    return jnp.concatenate(
        [packed_ref[pl.ds(q * ROWS + start, 8), 3 * BL :] for q in range(4)], axis=1
    )


def deposit(own, own_code, other, other_code):
    total = None
    for amount in (0, 1, 2, -1, -2):
        picked = jnp.where(own_code == float(amount), own, 0.0) + jnp.where(
            other_code == float(amount + 8), other, 0.0
        )
        if amount:
            picked = pltpu.roll(picked, amount % N, 1)
        total = picked if total is None else total + picked
    return total


def omega_kernel(s, *refs):
    own_ref = refs[0]
    packed = refs[1:5]
    early = refs[5:9] if s == 0 else (None,) * 4
    out_ref, far_ref = refs[-2:]
    for plane in range(2):
        other_ref = packed[2 + plane]
        ids = other_ref[2 * BL + s : 2 * BL + s + 1, 0:BL].astype(jnp.int32)
        parts = parts_of(other_ref[s * BL : (s + 1) * BL, 0 : 3 * BL])
        for q in range(4):
            chosen = chosen_rows(ids, q)
            total = None
            for part in parts:
                term = jnp.dot(chosen, part, preferred_element_type=jnp.float32)
                total = term if total is None else total + term
            for c in range(3):
                far_ref[c, :, q * BL : (q + 1) * BL] = total[:, c * BL : (c + 1) * BL]

        @pl.loop(0, ROWS // 8)
        def _(step, plane=plane):
            start = pl.multiple_of(step * 8, 8)
            rows = pl.ds(start, 8)
            own_code = code_rows(s, early[plane], packed[plane], start)
            other_code = code_rows(s, early[2 + plane], packed[2 + plane], start)
            for c in range(3):
                out_ref[c, plane, rows, :] = deposit(
                    own_ref[s, c, plane, rows, :], own_code, far_ref[c, rows, :], other_code
                )


def omega_of(s, *args):
    def body(*refs):
        omega_kernel(s, *refs)

    return pl.pallas_call(
        body,
        out_shape=jax.ShapeDtypeStruct((3, 2, ROWS, N), jnp.float32),
        in_specs=[pl.BlockSpec(memory_space=pltpu.VMEM)] * len(args),
        out_specs=pl.BlockSpec(memory_space=pltpu.VMEM),
        scratch_shapes=[pltpu.VMEM((3, ROWS, N), jnp.float32)],
        compiler_params=pltpu.CompilerParams(vmem_limit_bytes=VMEM_LIMIT),
        cost_estimate=pl.CostEstimate(flops=300_000_000, bytes_accessed=6_000_000, transcendentals=0),
        name="omega",
    )(*args)


SUBLANE = (0, 4, 12)


def first_kernel(s, *refs):
    own_refs, far_refs = refs[0:2], refs[2:4]
    packed = refs[4:8] if s else (None,) * 4
    forward_ref, table_ref, lam_ref, u_ref, ends_ref, x_ref, h_ref = refs[-7:]
    for plane, other in ((0, 0), (1, 3)):
        own_ref, other_ref = own_refs[plane], far_refs[plane]

        @pl.loop(0, ROWS // 8)
        def _(step, plane=plane, other=other, own_ref=own_ref, other_ref=other_ref):
            start = pl.multiple_of(step * 8, 8)
            rows = pl.ds(start, 8)
            own_code = code_rows(s, own_ref, packed[plane], start)
            other_code = code_rows(s, other_ref, packed[2 + plane], start)
            for c in range(3):
                own = own_ref[c, rows, :]
                far = other_ref[c, rows, :]
                here = deposit(own, own_code, far, other_code)
                there = deposit(far, other_code, own, own_code)
                lam_ref[c, plane, rows, :] = here
                for place, value in ((plane + 1, here), (other, there)):
                    base = (c * 4 + place) * ROWS
                    at = pl.ds(pl.multiple_of(base + start, 8), 8)
                    x_ref[at, :H] = value[:, :H] + value[:, H:]
                    x_ref[at, H:] = value[:, :H] - value[:, H:]

    for block in range(2):
        lanes = pl.ds(block * H, H)
        out = dot3(x_ref[:, lanes], forward_ref, block)
        for c in range(3):
            for place in range(4):
                base = (c * 4 + place) * ROWS
                for part in range(2):
                    h_ref[block * 2 + part, pl.ds(SUBLANE[c] + place, ROWS, stride=16), :] = out[
                        base : base + ROWS, part * BL : (part + 1) * BL
                    ]

    r = [jnp.broadcast_to(table_ref[R_ROW, :, q * BL : (q + 1) * BL], (16, BL)) for q in range(4)]
    zero = jnp.zeros((16, BL), jnp.float32)

    def ahead(y, carry):
        at = pl.ds(pl.multiple_of(y * 16, 16), 16)
        new = []
        for q in range(4):
            value = h_ref[q, at, :] + r[q] * carry[q]
            u_ref[q, at, :] = value
            new.append(value)
        return tuple(new)

    u_end = lax.fori_loop(0, ROWS, ahead, (zero,) * 4, unroll=8)

    def back(i, carry):
        y = ROWS - 1 - i
        at = pl.ds(pl.multiple_of(y * 16, 16), 16)
        new = [u_ref[q, at, :] + r[q] * carry[q] for q in range(4)]
        return (*new, carry[4] + new[0])

    w_end = lax.fori_loop(0, ROWS, back, (zero,) * 5, unroll=8)
    for q in range(4):
        lanes = pl.ds(q * BL, BL)
        ends_ref[0:8, lanes] = u_end[q][0:8]
        ends_ref[8:12, lanes] = u_end[q][12:16]
        ends_ref[12:20, lanes] = w_end[q][0:8]
        ends_ref[20:24, lanes] = w_end[q][12:16]
    lane = lax.broadcasted_iota(jnp.int32, (16, BL), 1)
    sub = lax.broadcasted_iota(jnp.int32, (16, BL), 0)
    sums = jnp.broadcast_to(w_end[4][:, 0:1], (16, BL))
    ends_ref[24:25, :] = jnp.zeros((1, N), jnp.float32)
    used = (lane == sub) & ((sub < 8) | (sub >= 12))
    ends_ref[24:25, 0:BL] = jnp.sum(jnp.where(used, sums, 0.0), axis=0, keepdims=True)


def first_of(s, *args):
    def body(*refs):
        first_kernel(s, *refs)

    return pl.pallas_call(
        body,
        out_shape=(
            jax.ShapeDtypeStruct((3, 2, ROWS, N), jnp.float32),
            jax.ShapeDtypeStruct((4, ROWS * 16, BL), jnp.float32),
            jax.ShapeDtypeStruct((25, N), jnp.float32),
        ),
        in_specs=[pl.BlockSpec(memory_space=pltpu.VMEM)] * len(args),
        out_specs=(pl.BlockSpec(memory_space=pltpu.VMEM),) * 3,
        scratch_shapes=[
            pltpu.VMEM((12 * ROWS, N), jnp.float32),
            pltpu.VMEM((4, ROWS * 16, BL), jnp.float32),
        ],
        compiler_params=pltpu.CompilerParams(vmem_limit_bytes=VMEM_LIMIT),
        cost_estimate=pl.CostEstimate(flops=3_000_000_000, bytes_accessed=8_000_000, transcendentals=0),
        name="first",
    )(*args)


def second_kernel(
    zero_u, zero_z, last, *refs
):
    ends_refs = refs[:GROUPS]
    u_ref, lam_ref, omega_ref, table_ref, inverse_ref = refs[GROUPS : GROUPS + 5]
    out_refs = refs[GROUPS + 5 : -2]
    y_ref, field_ref = refs[-2:]
    me = lax.axis_index("pencil")
    u_in = [[jnp.zeros((8, BL), jnp.float32)] * 2 for _ in range(4)]
    w_in = [[jnp.zeros((8, BL), jnp.float32)] * 2 for _ in range(4)]
    u_sum = [jnp.zeros((8, BL), jnp.float32)] * 2
    w_sum = [jnp.zeros((8, BL), jnp.float32)] * 2
    z_row = jnp.zeros((1, BL), jnp.float32)
    for step in range(GROUPS):
        ends_ref = ends_refs[step]
        who = (me ^ step) - me & (GROUPS - 1)
        for q in range(4):
            lanes = pl.ds(q * BL, BL)
            uu = table_ref[CUU_ROW + who, :, lanes]
            ww = table_ref[CWW_ROW + who, :, lanes]
            wu = table_ref[CWU_ROW + who, :, lanes]
            for g in range(2):
                u = ends_ref[4 * g : 4 * g + 8, lanes]
                w = ends_ref[12 + 4 * g : 20 + 4 * g, lanes]
                u_in[q][g] = u_in[q][g] + uu * u
                w_in[q][g] = w_in[q][g] + (ww * w + wu * u)
                if q == 0:
                    u_sum[g] = u_sum[g] + u
                    w_sum[g] = w_sum[g] + w
        z_row = z_row + ends_ref[24:25, 0:BL]
    lane = lax.broadcasted_iota(jnp.int32, (8, BL), 1)
    sub = lax.broadcasted_iota(jnp.int32, (8, BL), 0)
    first_lane = lane == 0
    mean = []
    for g in range(2):
        u_in[0][g] = u_in[0][g] + jnp.where(first_lane, zero_u * w_sum[g], 0.0)
        mean.append(jnp.where(first_lane, u_sum[g] * (1.0 / N), 0.0))
        mine = jnp.where(lane == sub + 8 * g, jnp.broadcast_to(z_row, (8, BL)), 0.0)
        z_total = jnp.broadcast_to(jnp.sum(mine, axis=1, keepdims=True), (8, BL))
        w_in[0][g] = w_in[0][g] + jnp.where(first_lane, zero_z * z_total, 0.0)

    r = [jnp.broadcast_to(table_ref[R_ROW, :, q * BL : (q + 1) * BL], (8, BL)) for q in range(4)]
    swap = [
        jnp.broadcast_to(table_ref[SWAP_ROW, :, q * BL : (q + 1) * BL], (8, BL)) for q in range(4)
    ]
    upper = sub < 4

    def emit(y, after, here, before):
        at = pl.ds(pl.multiple_of(y * 8, 8), 8)
        at_b = pl.ds(pl.multiple_of(ROWS * 8 + y * 8, 8), 8)
        for q in range(4):
            slope0 = 0.5 * (after[2 * q] - before[2 * q])
            slope1 = 0.5 * (after[2 * q + 1] - before[2 * q + 1])
            turned = swap[q] * here[2 * (q ^ 1)]
            lanes = pl.ds(q * BL, BL)
            y_ref[at, lanes] = jnp.where(upper, here[2 * q], slope1 - turned)
            y_ref[at_b, lanes] = slope0

    def back(i, carry):
        y = ROWS - 1 - i
        after, here = carry[:8], carry[8:]
        new = []
        for q in range(4):
            power = table_ref[y, :, q * BL : (q + 1) * BL]
            for g in range(2):
                at = pl.ds(pl.multiple_of(y * 16 + 8 * g, 8), 8)
                value = u_ref[q, at, :] + power * u_in[q][g]
                if q == 0:
                    value = value - (y + 1).astype(jnp.float32) * mean[g]
                new.append(value + r[q] * here[2 * q + g])
        emit(y + 1, after, here, new)
        return (*here, *new)

    edge = tuple(w_in[q][g] for q in range(4) for g in range(2))
    new = []
    for q in range(4):
        power = table_ref[ROWS - 1, :, q * BL : (q + 1) * BL]
        for g in range(2):
            value = u_ref[q, (ROWS - 1) * 16 + 8 * g : (ROWS - 1) * 16 + 8 * g + 8, :]
            value = value + power * u_in[q][g]
            if q == 0:
                value = value - float(ROWS) * mean[g]
            new.append(value + r[q] * edge[2 * q + g])
    carry = lax.fori_loop(1, ROWS, back, (*edge, *new), unroll=3)
    after, here = carry[:8], carry[8:]
    before = [u_in[q][g] + r[q] * here[2 * q + g] for q in range(4) for g in range(2)]
    emit(jnp.int32(0), after, here, before)

    even = dot3(y_ref[:, :H], inverse_ref, 0)
    odd = dot3(y_ref[:, H:], inverse_ref, 1)
    for part in range(2):
        lanes = slice(part * BL, (part + 1) * BL)
        field_ref[part] = even[:, lanes] + odd[:, lanes]
        field_ref[2 + part] = even[:, lanes] - odd[:, lanes]

    @pl.loop(0, ROWS // 8)
    def _(step):
        start = pl.multiple_of(step * 8, 8)
        rows = pl.ds(start, 8)

        def load(base):
            parts = [
                field_ref[q, pl.ds(start * 8 + base, 8, stride=8), :]
                for q in range(4)
            ]
            return jnp.concatenate(parts, axis=1)

        g = []
        for place in range(4):
            psi = load(place)
            gx = load(4 + place)
            gz = -load(ROWS * 8 + place)
            gy = 0.5 * (pltpu.roll(psi, N - 1, 1) - pltpu.roll(psi, 1, 1))
            g.append((gx, gy, gz))
        for plane in range(2):
            here = g[plane + 1]
            w = [omega_ref[c, plane, rows, :] for c in range(3)]
            cross = (
                w[1] * here[2] - w[2] * here[1],
                w[2] * here[0] - w[0] * here[2],
                w[0] * here[1] - w[1] * here[0],
            )
            for c in range(3):
                slope = 0.5 * (g[plane + 2][c] - g[plane][c])
                new = lam_ref[c, plane, rows, :] + TIME_STEP * (cross[c] + w[0] * slope)
                if last:
                    out_refs[0][c, plane, rows, :] = new
                else:
                    out_refs[plane][c, rows, :] = new


def second_of(t, last, *args):
    def body(*refs):
        second_kernel(t["zero_u"], t["zero_z"], last, *refs)

    if last:
        shapes = (jax.ShapeDtypeStruct((3, 2, ROWS, N), jnp.float32),)
    else:
        shapes = (jax.ShapeDtypeStruct((3, ROWS, N), jnp.float32),) * 2
    return pl.pallas_call(
        body,
        out_shape=shapes,
        in_specs=[pl.BlockSpec(memory_space=pltpu.VMEM)] * (GROUPS + 5),
        out_specs=(pl.BlockSpec(memory_space=pltpu.VMEM),) * len(shapes),
        scratch_shapes=[
            pltpu.VMEM((ROWS * 16, N), jnp.float32),
            pltpu.VMEM((4, ROWS * 16, BL), jnp.float32),
        ],
        compiler_params=pltpu.CompilerParams(vmem_limit_bytes=VMEM_LIMIT),
        cost_estimate=pl.CostEstimate(flops=4_000_000_000, bytes_accessed=8_000_000, transcendentals=0),
        name="second",
    )(*args)


def shifted(value, axis, by):
    count = lax.axis_size(axis)
    return lax.ppermute(value, axis, [(i, (i + by) % count) for i in range(count)])


def neighbours(lower_plane, upper_plane):
    return shifted(upper_plane, "slab", 1), shifted(lower_plane, "slab", -1)


def crossed(value, mask):
    return lax.ppermute(value, "pencil", [(i, i ^ mask) for i in range(GROUPS)])


def gathered(ends):
    far = [ends] + [crossed(ends, 2 * d) for d in (1, 2, 3)]
    out = []
    for value in far:
        out += [value, crossed(value, 1)]
    return out


def shards(adjoint_vort, omega_ckpt, cell_shift, move_count, move_blocks):
    t = tables()
    forward, inverse = halves(t["forward"]), halves(t["inverse"])
    rows = [t["rpow"], t["cuu"], t["cww"], t["cwu"], t["r"][None], t["swap"][None]]
    table = jnp.asarray(np.concatenate(rows)[:, None], jnp.float32)

    lows = early_of(move_count, move_blocks, cell_shift, adjoint_vort)
    far = neighbours(*lows)
    packed = packed_of(move_count, move_blocks, cell_shift, omega_ckpt)
    far_packed = neighbours(*packed)
    for s in range(2):
        extra = () if s == 0 else (*packed, *far_packed)
        if s:
            far = neighbours(*lows)
            omega = omega_of(s, omega_ckpt, *packed, *far_packed)
            far, omega = lax.optimization_barrier((far, omega))
        else:
            omega = omega_of(s, omega_ckpt, *packed, *far_packed, *lows, *far)
        lam_r, u, ends = first_of(s, *lows, *far, *extra, forward, table)
        out = second_of(t, s == 1, *gathered(ends), u, lam_r, omega, table, inverse)
        if s == 0:
            lows = out
    return out[0]


def solution(mesh):
    return jax.shard_map(
        shards,
        mesh=mesh,
        in_specs=(
            P(None, "slab", "pencil", None),
            P(None, None, "slab", "pencil", None),
            P(None, "slab", "pencil", None),
            P(None, "slab", "pencil", None),
            P(None, "slab", "pencil", None, None),
        ),
        out_specs=P(None, "slab", "pencil", None),
        check_vma=False,
    )
```

```python
import jax
import jax.numpy as jnp
import numpy as np
from jax import lax
from jax.experimental import pallas as pl
from jax.experimental.pallas import tpu as pltpu
from jax.sharding import PartitionSpec as P


N = 512
H = 256
ROWS = 64
GROUPS = 8
BL = 128
TIME_STEP = 0.25
VMEM_LIMIT = 16 * 1024 * 1024
WIDE_LIMIT = 60 * 1024 * 1024
CUU_ROW = ROWS
CWW_ROW = CUU_ROW + GROUPS
CWU_ROW = CWW_ROW + GROUPS
R_ROW = CWU_ROW + GROUPS
SWAP_ROW = R_ROW + 1


def lane_wave():
    m = np.arange(128)
    return np.concatenate([2 * m, np.where(m == 0, 256, 2 * m), 2 * m + 1, 2 * m + 1])


def tables():
    wave = lane_wave()
    z = np.arange(H)
    angle = 2 * np.pi * (wave[:, None] * z[None, :] % N) / N
    is_sin = np.zeros(N, bool)
    is_sin[129:256] = True
    is_sin[384:] = True
    basis = np.where(is_sin[:, None], np.sin(angle), np.cos(angle))
    forward = np.stack([basis[:H].T, basis[H:].T])
    lam = 4 * np.sin(np.pi * wave / N) ** 2
    r = 1 + lam / 2 - np.sqrt(lam + lam * lam / 4)
    norm = np.where((wave == 0) | (wave == 256), 1.0, 2.0) / N
    inverse = basis * (norm * r)[:, None]
    inverse = np.stack([inverse[:H], inverse[H:]])
    sigma = np.sin(2 * np.pi * wave / N)
    sigma[128] = 0.0
    sigma[0] = 0.0
    swap = sigma.copy()
    swap[128:256] *= -1
    swap[384:] *= -1
    rpow = r[None, :] ** (np.arange(ROWS)[:, None] + 1)

    rs = np.where(wave == 0, 0.5, r)
    rho = rs**ROWS
    wrap = 1 / (1 - rho**GROUPS)
    step = np.arange(GROUPS)
    up = np.where(step == 0, GROUPS, GROUPS - step)
    down = np.where(step == 0, GROUPS, step)
    cuu = rho[None, :] ** (up[:, None] - 1) * wrap
    cww = rho[None, :] ** (down[:, None] - 1) * wrap
    kappa = rs * (1 - rs ** (2 * ROWS)) / (1 - rs**2)
    cwu = np.zeros((GROUPS, N))
    for a in range(GROUPS):
        for b in range(GROUPS):
            cwu[(a + b) % GROUPS] += kappa * cww[a] * cuu[b]
    tri = ROWS * (ROWS + 1) // 2
    pyr = sum(tri - y * (y + 1) // 2 for y in range(ROWS))
    left, right = [], []
    row, rhs = np.zeros(17), np.zeros(24)
    row[16] = N
    rhs[:8] = 1
    left.append(row)
    right.append(rhs)
    for m in range(8):
        row, rhs = np.zeros(17), np.zeros(24)
        row[(m + 1) % 8] += 1
        row[m] -= 1
        row[16] = ROWS
        rhs[m] = 1
        left.append(row)
        right.append(rhs)
        row, rhs = np.zeros(17), np.zeros(24)
        row[8 + (m - 1) % 8] += 1
        row[8 + m] -= 1
        row[m] -= ROWS
        row[16] = tri
        rhs[8 + m] = 1
        left.append(row)
        right.append(rhs)
    row, rhs = np.zeros(17), np.zeros(24)
    row[:8] = ROWS
    row[16] = -8 * tri
    rhs[8:16] = -1
    left.append(row)
    right.append(rhs)
    row, rhs = np.zeros(17), np.zeros(24)
    row[:8] = tri
    row[8:16] = ROWS
    row[16] = -8 * pyr
    rhs[16:] = -1
    left.append(row)
    right.append(rhs)
    answer = np.linalg.lstsq(np.array(left), np.array(right), rcond=None)[0]
    cuu[:, 0] = answer[0, :8]
    cww[:, 0] = answer[8, 8:16]
    cwu[:, 0] = answer[8, :8]
    zero_u = answer[0, 8]
    zero_z = answer[8, 16]
    return {
        "forward": forward,
        "inverse": inverse,
        "swap": swap,
        "rpow": rpow,
        "r": r,
        "cuu": cuu,
        "cww": cww,
        "cwu": cwu,
        "zero_u": float(zero_u),
        "zero_z": float(zero_z),
    }


def halves(matrix):
    full = np.asarray(matrix, np.float32)
    high = full.astype(jnp.bfloat16)
    low = (full - high.astype(np.float32)).astype(jnp.bfloat16)
    return jnp.asarray(np.stack([high, low]))


def split(x):
    high = x.astype(jnp.bfloat16)
    return high, (x - high.astype(jnp.float32)).astype(jnp.bfloat16)


def dot3(x, matrix_ref, block):
    high, low = split(x)
    first = matrix_ref[0, block]
    second = matrix_ref[1, block]
    out = jnp.dot(high, first, preferred_element_type=jnp.float32)
    out = out + jnp.dot(low, first, preferred_element_type=jnp.float32)
    return out + jnp.dot(high, second, preferred_element_type=jnp.float32)


def live_ids(count_ref, blocks_ref, s, direction):
    slot = lax.broadcasted_iota(jnp.int32, (1, BL), 1)
    ids = blocks_ref[s, 0, 0, direction : direction + 1, :]
    return jnp.where(slot < count_ref[s, 0, 0, direction], ids, -8)


def moved_of(ids):
    row_id = lax.broadcasted_iota(jnp.int32, (ROWS, BL), 0)
    lane_block = lax.broadcasted_iota(jnp.int32, (N, BL), 0) // BL
    rows = jnp.where(jnp.broadcast_to(ids >> 2, (ROWS, BL)) == row_id, 1.0, 0.0)
    lanes = jnp.where(jnp.broadcast_to(ids & 3, (N, BL)) == lane_block, 1.0, 0.0)
    return lax.dot_general(
        rows.astype(jnp.bfloat16),
        lanes.astype(jnp.bfloat16),
        (((1,), (1,)), ((), ())),
        preferred_element_type=jnp.float32,
    )


def early_kernel(count_hbm, blocks_hbm, shift_hbm, lam_hbm, low_ref, high_ref, count_ref, blocks_ref, shift_ref, sem):
    copies = [
        pltpu.make_async_copy(count_hbm, count_ref, sem.at[0]),
        pltpu.make_async_copy(blocks_hbm.at[0], blocks_ref, sem.at[1]),
        pltpu.make_async_copy(shift_hbm.at[0], shift_ref, sem.at[2]),
        pltpu.make_async_copy(lam_hbm.at[:, 0], low_ref.at[pl.ds(0, 3)], sem.at[3]),
        pltpu.make_async_copy(lam_hbm.at[:, 1], high_ref.at[pl.ds(0, 3)], sem.at[4]),
    ]
    for copy in copies:
        copy.start()
    for copy in copies[:3]:
        copy.wait()
    slot = lax.broadcasted_iota(jnp.int32, (1, BL), 1)
    for plane, out_ref in ((0, low_ref), (1, high_ref)):
        direction = 1 - plane
        ids = blocks_ref[0, 0, direction : direction + 1, :]
        ids = jnp.where(slot < count_ref[0, 0, 0, direction], ids, -8)
        out_ref[3] = shift_ref[plane].astype(jnp.float32) + 8.0 * moved_of(ids)
    for copy in copies[3:]:
        copy.wait()


def early_of(count, blocks, shifts, lam):
    return pl.pallas_call(
        early_kernel,
        out_shape=(jax.ShapeDtypeStruct((4, ROWS, N), jnp.float32),) * 2,
        in_specs=[pl.BlockSpec(memory_space=pltpu.HBM)] * 4,
        out_specs=(pl.BlockSpec(memory_space=pltpu.VMEM),) * 2,
        scratch_shapes=[
            pltpu.SMEM(count.shape, jnp.int32),
            pltpu.VMEM(blocks.shape[1:], jnp.int32),
            pltpu.VMEM((2, ROWS, N), jnp.int32),
            pltpu.SemaphoreType.DMA((5,)),
        ],
        compiler_params=pltpu.CompilerParams(vmem_limit_bytes=WIDE_LIMIT),
        cost_estimate=pl.CostEstimate(flops=40_000_000, bytes_accessed=1_000_000, transcendentals=0),
        name="early",
    )(count, blocks, shifts, lam)


def parts_of(x):
    high = x.astype(jnp.bfloat16)
    rest = x - high.astype(jnp.float32)
    middle = rest.astype(jnp.bfloat16)
    return high, middle, (rest - middle.astype(jnp.float32)).astype(jnp.bfloat16)


def chosen_rows(ids, q):
    row_id = lax.broadcasted_iota(jnp.int32, (ROWS, BL), 0)
    wide = jnp.broadcast_to(ids, (ROWS, BL))
    hit = ((wide >> 2) == row_id) & ((wide & 3) == q)
    return jnp.where(hit, 1.0, 0.0).astype(jnp.bfloat16)


def pack_kernel(count_ref, blocks_ref, shift_ref, omega_ref, *out_refs):
    for s in range(2):
        for plane in range(2):
            out_ref = out_refs[2 * s + plane]
            out_ref[BL:, :] = jnp.zeros((8, out_ref.shape[1]), jnp.float32)
            ids = live_ids(count_ref, blocks_ref, s, 1 - plane)
            out_ref[BL : BL + 1, 0:BL] = ids.astype(jnp.float32)
            total = jnp.zeros((BL, 3 * BL), jnp.float32)
            for q in range(4):
                chosen = chosen_rows(ids, q)
                lanes = slice(q * BL, (q + 1) * BL)
                x = jnp.concatenate([omega_ref[s, c, plane, :, lanes] for c in range(3)], axis=1)
                for part in parts_of(x):
                    total = total + lax.dot_general(
                        chosen, part, (((0,), (0,)), ((), ())), preferred_element_type=jnp.float32
                    )
            out_ref[0:BL, 0 : 3 * BL] = total
            if s == 1:
                code = shift_ref[1, plane].astype(jnp.float32) + 8.0 * moved_of(ids)
                for q in range(4):
                    rows = slice((q % 2) * ROWS, (q % 2 + 1) * ROWS)
                    lanes = slice((3 + q // 2) * BL, (4 + q // 2) * BL)
                    out_ref[rows, lanes] = code[:, q * BL : (q + 1) * BL]


def packed_of(count, blocks, shifts, omega):
    out = pl.pallas_call(
        pack_kernel,
        out_shape=(jax.ShapeDtypeStruct((BL + 8, 3 * BL), jnp.float32),) * 2
        + (jax.ShapeDtypeStruct((BL + 8, 5 * BL), jnp.float32),) * 2,
        in_specs=[
            pl.BlockSpec(memory_space=pltpu.SMEM),
            pl.BlockSpec(memory_space=pltpu.VMEM),
            pl.BlockSpec(memory_space=pltpu.VMEM),
            pl.BlockSpec(memory_space=pltpu.VMEM),
        ],
        out_specs=(pl.BlockSpec(memory_space=pltpu.VMEM),) * 4,
        compiler_params=pltpu.CompilerParams(vmem_limit_bytes=VMEM_LIMIT),
        cost_estimate=pl.CostEstimate(flops=300_000_000, bytes_accessed=3_000_000, transcendentals=0),
        name="pack",
    )(count, blocks, shifts, omega)
    return out[:2], out[2:]


def summed(refs, index):
    value = refs[0][index]
    for ref in refs[1:]:
        value = value + ref[index]
    return value


def code_rows(s, refs, start):
    if s == 0:
        return summed(refs, (3, pl.ds(start, 8), slice(None)))
    parts = []
    for q in range(4):
        rows = pl.ds((q % 2) * ROWS + start, 8)
        parts.append(summed(refs, (rows, slice((3 + q // 2) * BL, (4 + q // 2) * BL))))
    return jnp.concatenate(parts, axis=1)


def deposit(own, own_code, other, other_code):
    total = None
    for amount in (0, 1, 2, -1, -2):
        picked = jnp.where(own_code == float(amount), own, 0.0) + jnp.where(
            other_code == float(amount + 8), other, 0.0
        )
        if amount:
            picked = pltpu.roll(picked, amount % N, 1)
        total = picked if total is None else total + picked
    return total


def omega_kernel(s, own_ref, own_codes, far_codes, far_packed, out_ref, far_ref):
    for plane in range(2):
        refs = far_packed[plane]
        ids = summed(refs, (slice(BL, BL + 1), slice(0, BL))).astype(jnp.int32)
        parts = parts_of(summed(refs, (slice(0, BL), slice(0, 3 * BL))))
        for q in range(4):
            chosen = chosen_rows(ids, q)
            total = None
            for part in parts:
                term = jnp.dot(chosen, part, preferred_element_type=jnp.float32)
                total = term if total is None else total + term
            for c in range(3):
                far_ref[c, :, q * BL : (q + 1) * BL] = total[:, c * BL : (c + 1) * BL]

        @pl.loop(0, ROWS // 8)
        def _(step, plane=plane):
            start = pl.multiple_of(step * 8, 8)
            rows = pl.ds(start, 8)
            own_code = code_rows(s, (own_codes[plane],), start)
            other_code = code_rows(s, far_codes[plane], start)
            for c in range(3):
                out_ref[c, plane, rows, :] = deposit(
                    own_ref[s, c, plane, rows, :], own_code, far_ref[c, rows, :], other_code
                )


def omega_of(s, own, own_codes, far_codes, far_packed):
    args, tree = jax.tree.flatten((own, own_codes, far_codes, far_packed))

    def body(*refs):
        omega_kernel(s, *jax.tree.unflatten(tree, refs[: len(args)]), *refs[len(args) :])

    return pl.pallas_call(
        body,
        out_shape=jax.ShapeDtypeStruct((3, 2, ROWS, N), jnp.float32),
        in_specs=[pl.BlockSpec(memory_space=pltpu.VMEM)] * len(args),
        out_specs=pl.BlockSpec(memory_space=pltpu.VMEM),
        scratch_shapes=[pltpu.VMEM((3, ROWS, N), jnp.float32)],
        compiler_params=pltpu.CompilerParams(vmem_limit_bytes=VMEM_LIMIT),
        cost_estimate=pl.CostEstimate(flops=300_000_000, bytes_accessed=6_000_000, transcendentals=0),
        name="omega",
    )(*args)


SUBLANE = (0, 4, 12)


def first_kernel(
    s, own_refs, far_refs, own_codes, far_codes, forward_ref, table_ref,
    lam_ref, u_ref, ends_ref, x_ref, h_ref,
):
    for plane, other in ((0, 0), (1, 3)):
        own_ref, other_ref = own_refs[plane], far_refs[plane]

        @pl.loop(0, ROWS // 8)
        def _(step, plane=plane, other=other, own_ref=own_ref, other_ref=other_ref):
            start = pl.multiple_of(step * 8, 8)
            rows = pl.ds(start, 8)
            own_code = code_rows(s, (own_codes[plane],), start)
            other_code = code_rows(s, far_codes[plane], start)
            for c in range(3):
                own = own_ref[c, rows, :]
                far = other_ref[c, rows, :]
                here = deposit(own, own_code, far, other_code)
                there = deposit(far, other_code, own, own_code)
                lam_ref[c, plane, rows, :] = here
                for place, value in ((plane + 1, here), (other, there)):
                    base = (c * 4 + place) * ROWS
                    at = pl.ds(pl.multiple_of(base + start, 8), 8)
                    x_ref[at, :H] = value[:, :H] + value[:, H:]
                    x_ref[at, H:] = value[:, :H] - value[:, H:]

    for block in range(2):
        lanes = pl.ds(block * H, H)
        out = dot3(x_ref[:, lanes], forward_ref, block)
        for c in range(3):
            for place in range(4):
                base = (c * 4 + place) * ROWS
                for part in range(2):
                    h_ref[block * 2 + part, pl.ds(SUBLANE[c] + place, ROWS, stride=16), :] = out[
                        base : base + ROWS, part * BL : (part + 1) * BL
                    ]

    r = [jnp.broadcast_to(table_ref[R_ROW, :, q * BL : (q + 1) * BL], (16, BL)) for q in range(4)]
    zero = jnp.zeros((16, BL), jnp.float32)

    def ahead(y, carry):
        at = pl.ds(pl.multiple_of(y * 16, 16), 16)
        new = []
        for q in range(4):
            value = h_ref[q, at, :] + r[q] * carry[q]
            u_ref[q, at, :] = value
            new.append(value)
        return tuple(new)

    u_end = lax.fori_loop(0, ROWS, ahead, (zero,) * 4, unroll=8)

    def back(i, carry):
        y = ROWS - 1 - i
        at = pl.ds(pl.multiple_of(y * 16, 16), 16)
        new = [u_ref[q, at, :] + r[q] * carry[q] for q in range(4)]
        return (*new, carry[4] + new[0])

    w_end = lax.fori_loop(0, ROWS, back, (zero,) * 5, unroll=8)
    for q in range(4):
        lanes = pl.ds(q * BL, BL)
        ends_ref[0:8, lanes] = u_end[q][0:8]
        ends_ref[8:12, lanes] = u_end[q][12:16]
        ends_ref[12:20, lanes] = w_end[q][0:8]
        ends_ref[20:24, lanes] = w_end[q][12:16]
    lane = lax.broadcasted_iota(jnp.int32, (16, BL), 1)
    sub = lax.broadcasted_iota(jnp.int32, (16, BL), 0)
    sums = jnp.broadcast_to(w_end[4][:, 0:1], (16, BL))
    ends_ref[24:25, :] = jnp.zeros((1, N), jnp.float32)
    used = (lane == sub) & ((sub < 8) | (sub >= 12))
    ends_ref[24:25, 0:BL] = jnp.sum(jnp.where(used, sums, 0.0), axis=0, keepdims=True)


def first_of(s, lows, far, own_codes, far_codes, forward, table):
    args, tree = jax.tree.flatten((lows, far, own_codes, far_codes, forward, table))

    def body(*refs):
        first_kernel(s, *jax.tree.unflatten(tree, refs[: len(args)]), *refs[len(args) :])

    return pl.pallas_call(
        body,
        out_shape=(
            jax.ShapeDtypeStruct((3, 2, ROWS, N), jnp.float32),
            jax.ShapeDtypeStruct((4, ROWS * 16, BL), jnp.float32),
            jax.ShapeDtypeStruct((25, N), jnp.float32),
        ),
        in_specs=[pl.BlockSpec(memory_space=pltpu.VMEM)] * len(args),
        out_specs=(pl.BlockSpec(memory_space=pltpu.VMEM),) * 3,
        scratch_shapes=[
            pltpu.VMEM((12 * ROWS, N), jnp.float32),
            pltpu.VMEM((4, ROWS * 16, BL), jnp.float32),
        ],
        compiler_params=pltpu.CompilerParams(vmem_limit_bytes=VMEM_LIMIT),
        cost_estimate=pl.CostEstimate(flops=3_000_000_000, bytes_accessed=8_000_000, transcendentals=0),
        name="first",
    )(*args)


def second_kernel(
    zero_u, zero_z, last, *refs
):
    ends_refs = refs[:GROUPS]
    u_ref, lam_ref, omega_ref, table_ref, inverse_ref = refs[GROUPS : GROUPS + 5]
    out_refs = refs[GROUPS + 5 : -2]
    y_ref, field_ref = refs[-2:]
    me = lax.axis_index("pencil")
    u_in = [[jnp.zeros((8, BL), jnp.float32)] * 2 for _ in range(4)]
    w_in = [[jnp.zeros((8, BL), jnp.float32)] * 2 for _ in range(4)]
    u_sum = [jnp.zeros((8, BL), jnp.float32)] * 2
    w_sum = [jnp.zeros((8, BL), jnp.float32)] * 2
    z_row = jnp.zeros((1, BL), jnp.float32)
    for step in range(GROUPS):
        ends_ref = ends_refs[step]
        who = (me ^ step) - me & (GROUPS - 1)
        for q in range(4):
            lanes = pl.ds(q * BL, BL)
            uu = table_ref[CUU_ROW + who, :, lanes]
            ww = table_ref[CWW_ROW + who, :, lanes]
            wu = table_ref[CWU_ROW + who, :, lanes]
            for g in range(2):
                u = ends_ref[4 * g : 4 * g + 8, lanes]
                w = ends_ref[12 + 4 * g : 20 + 4 * g, lanes]
                u_in[q][g] = u_in[q][g] + uu * u
                w_in[q][g] = w_in[q][g] + (ww * w + wu * u)
                if q == 0:
                    u_sum[g] = u_sum[g] + u
                    w_sum[g] = w_sum[g] + w
        z_row = z_row + ends_ref[24:25, 0:BL]
    lane = lax.broadcasted_iota(jnp.int32, (8, BL), 1)
    sub = lax.broadcasted_iota(jnp.int32, (8, BL), 0)
    first_lane = lane == 0
    mean = []
    for g in range(2):
        u_in[0][g] = u_in[0][g] + jnp.where(first_lane, zero_u * w_sum[g], 0.0)
        mean.append(jnp.where(first_lane, u_sum[g] * (1.0 / N), 0.0))
        mine = jnp.where(lane == sub + 8 * g, jnp.broadcast_to(z_row, (8, BL)), 0.0)
        z_total = jnp.broadcast_to(jnp.sum(mine, axis=1, keepdims=True), (8, BL))
        w_in[0][g] = w_in[0][g] + jnp.where(first_lane, zero_z * z_total, 0.0)

    r = [jnp.broadcast_to(table_ref[R_ROW, :, q * BL : (q + 1) * BL], (8, BL)) for q in range(4)]
    swap = [
        jnp.broadcast_to(table_ref[SWAP_ROW, :, q * BL : (q + 1) * BL], (8, BL)) for q in range(4)
    ]
    upper = sub < 4

    def emit(y, after, here, before):
        at = pl.ds(pl.multiple_of(y * 8, 8), 8)
        at_b = pl.ds(pl.multiple_of(ROWS * 8 + y * 8, 8), 8)
        for q in range(4):
            slope0 = 0.5 * (after[2 * q] - before[2 * q])
            slope1 = 0.5 * (after[2 * q + 1] - before[2 * q + 1])
            turned = swap[q] * here[2 * (q ^ 1)]
            lanes = pl.ds(q * BL, BL)
            y_ref[at, lanes] = jnp.where(upper, here[2 * q], slope1 - turned)
            y_ref[at_b, lanes] = slope0

    def back(i, carry):
        y = ROWS - 1 - i
        after, here = carry[:8], carry[8:]
        new = []
        for q in range(4):
            power = table_ref[y, :, q * BL : (q + 1) * BL]
            for g in range(2):
                at = pl.ds(pl.multiple_of(y * 16 + 8 * g, 8), 8)
                value = u_ref[q, at, :] + power * u_in[q][g]
                if q == 0:
                    value = value - (y + 1).astype(jnp.float32) * mean[g]
                new.append(value + r[q] * here[2 * q + g])
        emit(y + 1, after, here, new)
        return (*here, *new)

    edge = tuple(w_in[q][g] for q in range(4) for g in range(2))
    new = []
    for q in range(4):
        power = table_ref[ROWS - 1, :, q * BL : (q + 1) * BL]
        for g in range(2):
            value = u_ref[q, (ROWS - 1) * 16 + 8 * g : (ROWS - 1) * 16 + 8 * g + 8, :]
            value = value + power * u_in[q][g]
            if q == 0:
                value = value - float(ROWS) * mean[g]
            new.append(value + r[q] * edge[2 * q + g])
    carry = lax.fori_loop(1, ROWS, back, (*edge, *new), unroll=3)
    after, here = carry[:8], carry[8:]
    before = [u_in[q][g] + r[q] * here[2 * q + g] for q in range(4) for g in range(2)]
    emit(jnp.int32(0), after, here, before)

    even = dot3(y_ref[:, :H], inverse_ref, 0)
    odd = dot3(y_ref[:, H:], inverse_ref, 1)
    for part in range(2):
        lanes = slice(part * BL, (part + 1) * BL)
        field_ref[part] = even[:, lanes] + odd[:, lanes]
        field_ref[2 + part] = even[:, lanes] - odd[:, lanes]

    @pl.loop(0, ROWS // 8)
    def _(step):
        start = pl.multiple_of(step * 8, 8)
        rows = pl.ds(start, 8)

        def load(base):
            parts = [
                field_ref[q, pl.ds(start * 8 + base, 8, stride=8), :]
                for q in range(4)
            ]
            return jnp.concatenate(parts, axis=1)

        g = []
        for place in range(4):
            psi = load(place)
            gx = load(4 + place)
            gz = -load(ROWS * 8 + place)
            gy = 0.5 * (pltpu.roll(psi, N - 1, 1) - pltpu.roll(psi, 1, 1))
            g.append((gx, gy, gz))
        for plane in range(2):
            here = g[plane + 1]
            w = [omega_ref[c, plane, rows, :] for c in range(3)]
            cross = (
                w[1] * here[2] - w[2] * here[1],
                w[2] * here[0] - w[0] * here[2],
                w[0] * here[1] - w[1] * here[0],
            )
            for c in range(3):
                slope = 0.5 * (g[plane + 2][c] - g[plane][c])
                new = lam_ref[c, plane, rows, :] + TIME_STEP * (cross[c] + w[0] * slope)
                if last:
                    out_refs[0][c, plane, rows, :] = new
                else:
                    out_refs[plane][c, rows, :] = new


def second_of(t, last, *args):
    def body(*refs):
        second_kernel(t["zero_u"], t["zero_z"], last, *refs)

    if last:
        shapes = (jax.ShapeDtypeStruct((3, 2, ROWS, N), jnp.float32),)
    else:
        shapes = (jax.ShapeDtypeStruct((3, ROWS, N), jnp.float32),) * 2
    return pl.pallas_call(
        body,
        out_shape=shapes,
        in_specs=[pl.BlockSpec(memory_space=pltpu.VMEM)] * (GROUPS + 5),
        out_specs=(pl.BlockSpec(memory_space=pltpu.VMEM),) * len(shapes),
        scratch_shapes=[
            pltpu.VMEM((ROWS * 16, N), jnp.float32),
            pltpu.VMEM((4, ROWS * 16, BL), jnp.float32),
        ],
        compiler_params=pltpu.CompilerParams(vmem_limit_bytes=VMEM_LIMIT),
        cost_estimate=pl.CostEstimate(flops=4_000_000_000, bytes_accessed=8_000_000, transcendentals=0),
        name="second",
    )(*args)


def shifted(value, axis, by):
    count = lax.axis_size(axis)
    return lax.ppermute(value, axis, [(i, (i + by) % count) for i in range(count)])


def neighbours(lower_plane, upper_plane):
    below = shifted(upper_plane, "slab", 1)
    above = shifted(lower_plane, "slab", -1)
    return below, above


FAR = ((15, 16), (31, 0))
RELAY_UP = ({15: 3, 31: 19}, {3: 16, 19: 0})
RELAY_DOWN = ({16: 28, 0: 12}, {28: 15, 12: 31})


def relayed(lower_plane, upper_plane):
    count = lax.axis_size("slab")
    up = [(i, (i + 1) % count) for i in range(count)]
    out = []
    for value, near, relay in (
        (upper_plane, [p for p in up if p not in FAR], RELAY_UP),
        (lower_plane, [(b, a) for a, b in up if (a, b) not in FAR], RELAY_DOWN),
    ):
        hop = lax.ppermute(value, "slab", list(relay[0].items()))
        direct = lax.ppermute(value, "slab", near)
        out.append((direct, lax.ppermute(hop, "slab", list(relay[1].items()))))
    return out


def crossed(value, mask):
    return lax.ppermute(value, "pencil", [(i, i ^ mask) for i in range(GROUPS)])


def gathered(ends):
    far = [ends] + [crossed(ends, 2 * d) for d in (1, 2, 3)]
    out = []
    for value in far:
        out += [value, crossed(value, 1)]
    return out


def steps(adjoint_vort, omega_ckpt, cell_shift, move_count, move_blocks):
    t = tables()
    forward, inverse = halves(t["forward"]), halves(t["inverse"])
    rows = [t["rpow"], t["cuu"], t["cww"], t["cwu"], t["r"][None], t["swap"][None]]
    table = jnp.asarray(np.concatenate(rows)[:, None], jnp.float32)

    lows = early_of(move_count, move_blocks, cell_shift, adjoint_vort)
    far = neighbours(*lows)
    packed = packed_of(move_count, move_blocks, cell_shift, omega_ckpt)
    far_packed = [relayed(*pair) for pair in packed]
    for s in range(2):
        if s == 0:
            own_codes, far_codes = lows, [(value,) for value in far]
            omega = omega_of(s, omega_ckpt, own_codes, far_codes, far_packed[0])
        else:
            far = neighbours(*lows)
            own_codes, far_codes = packed[1], far_packed[1]
            omega = omega_of(s, omega_ckpt, own_codes, far_codes, far_packed[1])
            far, omega = lax.optimization_barrier((far, omega))
        lam_r, u, ends = first_of(s, lows, far, own_codes, far_codes, forward, table)
        out = second_of(t, s == 1, *gathered(ends), u, lam_r, omega, table, inverse)
        if s == 0:
            lows = out
    return out[0]


def solution(mesh):
    return jax.shard_map(
        steps,
        mesh=mesh,
        in_specs=(
            P(None, "slab", "pencil", None),
            P(None, None, "slab", "pencil", None),
            P(None, "slab", "pencil", None),
            P(None, "slab", "pencil", None),
            P(None, "slab", "pencil", None, None),
        ),
        out_specs=P(None, "slab", "pencil", None),
        check_vma=False,
    )
```

```python
import jax
import jax.numpy as jnp
import numpy as np
from jax import lax
from jax.experimental import pallas as pl
from jax.experimental.pallas import tpu as pltpu
from jax.sharding import PartitionSpec as P


N = 512
H = 256
ROWS = 64
GROUPS = 8
BL = 128
TIME_STEP = 0.25
VMEM_LIMIT = 16 * 1024 * 1024
WIDE_LIMIT = 60 * 1024 * 1024
CUU_ROW = ROWS
CWW_ROW = CUU_ROW + GROUPS
CWU_ROW = CWW_ROW + GROUPS
R_ROW = CWU_ROW + GROUPS
SWAP_ROW = R_ROW + 1


def lane_wave():
    m = np.arange(128)
    return np.concatenate([2 * m, np.where(m == 0, 256, 2 * m), 2 * m + 1, 2 * m + 1])


def tables():
    wave = lane_wave()
    z = np.arange(H)
    angle = 2 * np.pi * (wave[:, None] * z[None, :] % N) / N
    is_sin = np.zeros(N, bool)
    is_sin[129:256] = True
    is_sin[384:] = True
    basis = np.where(is_sin[:, None], np.sin(angle), np.cos(angle))
    forward = np.stack([basis[:H].T, basis[H:].T])
    lam = 4 * np.sin(np.pi * wave / N) ** 2
    r = 1 + lam / 2 - np.sqrt(lam + lam * lam / 4)
    norm = np.where((wave == 0) | (wave == 256), 1.0, 2.0) / N
    inverse = basis * (norm * r)[:, None]
    inverse = np.stack([inverse[:H], inverse[H:]])
    sigma = np.sin(2 * np.pi * wave / N)
    sigma[128] = 0.0
    sigma[0] = 0.0
    swap = sigma.copy()
    swap[128:256] *= -1
    swap[384:] *= -1
    rpow = r[None, :] ** (np.arange(ROWS)[:, None] + 1)

    rs = np.where(wave == 0, 0.5, r)
    rho = rs**ROWS
    wrap = 1 / (1 - rho**GROUPS)
    step = np.arange(GROUPS)
    up = np.where(step == 0, GROUPS, GROUPS - step)
    down = np.where(step == 0, GROUPS, step)
    cuu = rho[None, :] ** (up[:, None] - 1) * wrap
    cww = rho[None, :] ** (down[:, None] - 1) * wrap
    kappa = rs * (1 - rs ** (2 * ROWS)) / (1 - rs**2)
    cwu = np.zeros((GROUPS, N))
    for a in range(GROUPS):
        for b in range(GROUPS):
            cwu[(a + b) % GROUPS] += kappa * cww[a] * cuu[b]
    tri = ROWS * (ROWS + 1) // 2
    pyr = sum(tri - y * (y + 1) // 2 for y in range(ROWS))
    left, right = [], []
    row, rhs = np.zeros(17), np.zeros(24)
    row[16] = N
    rhs[:8] = 1
    left.append(row)
    right.append(rhs)
    for m in range(8):
        row, rhs = np.zeros(17), np.zeros(24)
        row[(m + 1) % 8] += 1
        row[m] -= 1
        row[16] = ROWS
        rhs[m] = 1
        left.append(row)
        right.append(rhs)
        row, rhs = np.zeros(17), np.zeros(24)
        row[8 + (m - 1) % 8] += 1
        row[8 + m] -= 1
        row[m] -= ROWS
        row[16] = tri
        rhs[8 + m] = 1
        left.append(row)
        right.append(rhs)
    row, rhs = np.zeros(17), np.zeros(24)
    row[:8] = ROWS
    row[16] = -8 * tri
    rhs[8:16] = -1
    left.append(row)
    right.append(rhs)
    row, rhs = np.zeros(17), np.zeros(24)
    row[:8] = tri
    row[8:16] = ROWS
    row[16] = -8 * pyr
    rhs[16:] = -1
    left.append(row)
    right.append(rhs)
    answer = np.linalg.lstsq(np.array(left), np.array(right), rcond=None)[0]
    cuu[:, 0] = answer[0, :8]
    cww[:, 0] = answer[8, 8:16]
    cwu[:, 0] = answer[8, :8]
    zero_u = answer[0, 8]
    zero_z = answer[8, 16]
    return {
        "forward": forward,
        "inverse": inverse,
        "swap": swap,
        "rpow": rpow,
        "r": r,
        "cuu": cuu,
        "cww": cww,
        "cwu": cwu,
        "zero_u": float(zero_u),
        "zero_z": float(zero_z),
    }


def halves(matrix):
    full = np.asarray(matrix, np.float32)
    high = full.astype(jnp.bfloat16)
    low = (full - high.astype(np.float32)).astype(jnp.bfloat16)
    return jnp.asarray(np.stack([high, low]))


def split(x):
    high = x.astype(jnp.bfloat16)
    return high, (x - high.astype(jnp.float32)).astype(jnp.bfloat16)


def dot3(x, matrix_ref, block):
    high, low = split(x)
    first = matrix_ref[0, block]
    second = matrix_ref[1, block]
    out = jnp.dot(high, first, preferred_element_type=jnp.float32)
    out = out + jnp.dot(low, first, preferred_element_type=jnp.float32)
    return out + jnp.dot(high, second, preferred_element_type=jnp.float32)


def live_ids(count_ref, blocks_ref, s, direction):
    slot = lax.broadcasted_iota(jnp.int32, (1, BL), 1)
    ids = blocks_ref[s, 0, 0, direction : direction + 1, :]
    return jnp.where(slot < count_ref[s, 0, 0, direction], ids, -8)


def moved_of(ids):
    row_id = lax.broadcasted_iota(jnp.int32, (ROWS, BL), 0)
    lane_block = lax.broadcasted_iota(jnp.int32, (N, BL), 0) // BL
    rows = jnp.where(jnp.broadcast_to(ids >> 2, (ROWS, BL)) == row_id, 1.0, 0.0)
    lanes = jnp.where(jnp.broadcast_to(ids & 3, (N, BL)) == lane_block, 1.0, 0.0)
    return lax.dot_general(
        rows.astype(jnp.bfloat16),
        lanes.astype(jnp.bfloat16),
        (((1,), (1,)), ((), ())),
        preferred_element_type=jnp.float32,
    )


def early_kernel(count_hbm, blocks_hbm, shift_hbm, lam_hbm, low_ref, high_ref, count_ref, blocks_ref, shift_ref, sem):
    copies = [
        pltpu.make_async_copy(count_hbm, count_ref, sem.at[0]),
        pltpu.make_async_copy(blocks_hbm.at[0], blocks_ref, sem.at[1]),
        pltpu.make_async_copy(shift_hbm.at[0], shift_ref, sem.at[2]),
        pltpu.make_async_copy(lam_hbm.at[:, 0], low_ref.at[pl.ds(0, 3)], sem.at[3]),
        pltpu.make_async_copy(lam_hbm.at[:, 1], high_ref.at[pl.ds(0, 3)], sem.at[4]),
    ]
    for copy in copies:
        copy.start()
    for copy in copies[:3]:
        copy.wait()
    slot = lax.broadcasted_iota(jnp.int32, (1, BL), 1)
    for plane, out_ref in ((0, low_ref), (1, high_ref)):
        direction = 1 - plane
        ids = blocks_ref[0, 0, direction : direction + 1, :]
        ids = jnp.where(slot < count_ref[0, 0, 0, direction], ids, -8)
        out_ref[3] = shift_ref[plane].astype(jnp.float32) + 8.0 * moved_of(ids)
    for copy in copies[3:]:
        copy.wait()


def early_of(count, blocks, shifts, lam):
    return pl.pallas_call(
        early_kernel,
        out_shape=(jax.ShapeDtypeStruct((4, ROWS, N), jnp.float32),) * 2,
        in_specs=[pl.BlockSpec(memory_space=pltpu.HBM)] * 4,
        out_specs=(pl.BlockSpec(memory_space=pltpu.VMEM),) * 2,
        scratch_shapes=[
            pltpu.SMEM(count.shape, jnp.int32),
            pltpu.VMEM(blocks.shape[1:], jnp.int32),
            pltpu.VMEM((2, ROWS, N), jnp.int32),
            pltpu.SemaphoreType.DMA((5,)),
        ],
        compiler_params=pltpu.CompilerParams(vmem_limit_bytes=WIDE_LIMIT),
        cost_estimate=pl.CostEstimate(flops=40_000_000, bytes_accessed=1_000_000, transcendentals=0),
        name="early",
    )(count, blocks, shifts, lam)


def parts_of(x):
    high = x.astype(jnp.bfloat16)
    rest = x - high.astype(jnp.float32)
    middle = rest.astype(jnp.bfloat16)
    return high, middle, (rest - middle.astype(jnp.float32)).astype(jnp.bfloat16)


def chosen_rows(ids, q):
    row_id = lax.broadcasted_iota(jnp.int32, (ROWS, BL), 0)
    wide = jnp.broadcast_to(ids, (ROWS, BL))
    hit = ((wide >> 2) == row_id) & ((wide & 3) == q)
    return jnp.where(hit, 1.0, 0.0).astype(jnp.bfloat16)


WIDTHS = (3 * BL, 5 * BL)
STARTS = (0, 3 * BL)


def pack_kernel(count_hbm, blocks_hbm, shift_hbm, omega_hbm, *refs):
    out_refs = refs[:6]
    count_ref, blocks_ref, shift_ref, omega_ref, sem = refs[6:]
    copies = [
        pltpu.make_async_copy(count_hbm, count_ref, sem.at[0]),
        pltpu.make_async_copy(blocks_hbm, blocks_ref, sem.at[1]),
        pltpu.make_async_copy(omega_hbm.at[0], omega_ref.at[0], sem.at[2]),
        pltpu.make_async_copy(omega_hbm.at[1], omega_ref.at[1], sem.at[3]),
        pltpu.make_async_copy(shift_hbm.at[1], shift_ref, sem.at[4]),
    ]
    for copy in copies:
        copy.start()
    for s in range(2):
        for copy in copies[:3] if s == 0 else copies[3:]:
            copy.wait()
        for plane in range(2):
            ids = live_ids(count_ref, blocks_ref, s, 1 - plane)
            total = jnp.zeros((BL, 3 * BL), jnp.float32)
            for q in range(4):
                chosen = chosen_rows(ids, q)
                lanes = slice(q * BL, (q + 1) * BL)
                x = jnp.concatenate([omega_ref[s, c, plane, :, lanes] for c in range(3)], axis=1)
                for part in parts_of(x):
                    total = total + lax.dot_general(
                        chosen, part, (((0,), (0,)), ((), ())), preferred_element_type=jnp.float32
                    )
            pieces = [total]
            if s == 1:
                code = shift_ref[plane].astype(jnp.float32) + 8.0 * moved_of(ids)
                part = [code[:, q * BL : (q + 1) * BL] for q in range(4)]
                pieces += [jnp.concatenate(part[0:2], axis=0), jnp.concatenate(part[2:4], axis=0)]
            message = jnp.concatenate(pieces, axis=1)
            for out_ref in (
                out_refs[plane].at[:, STARTS[s] : STARTS[s] + WIDTHS[s]],
                out_refs[2 + 2 * s + plane],
            ):
                out_ref[0:BL, :] = message
                out_ref[BL:, :] = jnp.zeros((8, WIDTHS[s]), jnp.float32)
                out_ref[BL : BL + 1, 0:BL] = ids.astype(jnp.float32)


def packed_of(count, blocks, shifts, omega):
    out = pl.pallas_call(
        pack_kernel,
        out_shape=tuple(
            jax.ShapeDtypeStruct((BL + 8, width), jnp.float32)
            for width in (8 * BL, 8 * BL, WIDTHS[0], WIDTHS[0], WIDTHS[1], WIDTHS[1])
        ),
        in_specs=[pl.BlockSpec(memory_space=pltpu.HBM)] * 4,
        out_specs=(pl.BlockSpec(memory_space=pltpu.VMEM),) * 6,
        scratch_shapes=[
            pltpu.SMEM(count.shape, jnp.int32),
            pltpu.VMEM(blocks.shape, jnp.int32),
            pltpu.VMEM((2, ROWS, N), jnp.int32),
            pltpu.VMEM(omega.shape, jnp.float32),
            pltpu.SemaphoreType.DMA((5,)),
        ],
        compiler_params=pltpu.CompilerParams(vmem_limit_bytes=WIDE_LIMIT),
        cost_estimate=pl.CostEstimate(flops=300_000_000, bytes_accessed=3_000_000, transcendentals=0),
        name="pack",
    )(count, blocks, shifts, omega)
    return out[0:2], out[2:4], out[4:6]


def summed(refs, index):
    value = refs[0][index]
    for ref in refs[1:]:
        value = value + ref[index]
    return value


def seen(s, refs):
    return (refs[0].at[:, STARTS[s] : STARTS[s] + WIDTHS[s]], *refs[1:])


def code_rows(s, refs, start):
    if s == 0:
        return summed(refs, (3, pl.ds(start, 8), slice(None)))
    refs = seen(s, refs)
    parts = []
    for q in range(4):
        rows = pl.ds((q % 2) * ROWS + start, 8)
        parts.append(summed(refs, (rows, slice((3 + q // 2) * BL, (4 + q // 2) * BL))))
    return jnp.concatenate(parts, axis=1)


def deposit(own, own_code, other, other_code):
    total = None
    for amount in (0, 1, 2, -1, -2):
        picked = jnp.where(own_code == float(amount), own, 0.0) + jnp.where(
            other_code == float(amount + 8), other, 0.0
        )
        if amount:
            picked = pltpu.roll(picked, amount % N, 1)
        total = picked if total is None else total + picked
    return total


def omega_kernel(s, own_ref, own_codes, far_codes, far_packed, out_ref, far_ref):
    for plane in range(2):
        refs = seen(s, far_packed[plane])
        ids = summed(refs, (slice(BL, BL + 1), slice(0, BL))).astype(jnp.int32)
        parts = parts_of(summed(refs, (slice(0, BL), slice(0, 3 * BL))))
        for q in range(4):
            chosen = chosen_rows(ids, q)
            total = None
            for part in parts:
                term = jnp.dot(chosen, part, preferred_element_type=jnp.float32)
                total = term if total is None else total + term
            for c in range(3):
                far_ref[c, :, q * BL : (q + 1) * BL] = total[:, c * BL : (c + 1) * BL]

        @pl.loop(0, ROWS // 8)
        def _(step, plane=plane):
            start = pl.multiple_of(step * 8, 8)
            rows = pl.ds(start, 8)
            own_code = code_rows(s, (own_codes[plane],), start)
            other_code = code_rows(s, far_codes[plane], start)
            for c in range(3):
                out_ref[c, plane, rows, :] = deposit(
                    own_ref[s, c, plane, rows, :], own_code, far_ref[c, rows, :], other_code
                )


def omega_of(s, own, own_codes, far_codes, far_packed):
    args, tree = jax.tree.flatten((own, own_codes, far_codes, far_packed))

    def body(*refs):
        omega_kernel(s, *jax.tree.unflatten(tree, refs[: len(args)]), *refs[len(args) :])

    return pl.pallas_call(
        body,
        out_shape=jax.ShapeDtypeStruct((3, 2, ROWS, N), jnp.float32),
        in_specs=[pl.BlockSpec(memory_space=pltpu.VMEM)] * len(args),
        out_specs=pl.BlockSpec(memory_space=pltpu.VMEM),
        scratch_shapes=[pltpu.VMEM((3, ROWS, N), jnp.float32)],
        compiler_params=pltpu.CompilerParams(vmem_limit_bytes=VMEM_LIMIT),
        cost_estimate=pl.CostEstimate(flops=300_000_000, bytes_accessed=6_000_000, transcendentals=0),
        name="omega",
    )(*args)


SUBLANE = (0, 4, 12)


def first_kernel(
    s, own_refs, far_refs, own_codes, far_codes, forward_ref, table_ref,
    lam_ref, u_ref, ends_ref, x_ref, h_ref,
):
    for plane, other in ((0, 0), (1, 3)):
        own_ref, other_ref = own_refs[plane], far_refs[plane]

        @pl.loop(0, ROWS // 8)
        def _(step, plane=plane, other=other, own_ref=own_ref, other_ref=other_ref):
            start = pl.multiple_of(step * 8, 8)
            rows = pl.ds(start, 8)
            own_code = code_rows(s, (own_codes[plane],), start)
            other_code = code_rows(s, far_codes[plane], start)
            for c in range(3):
                own = own_ref[c, rows, :]
                far = other_ref[c, rows, :]
                here = deposit(own, own_code, far, other_code)
                there = deposit(far, other_code, own, own_code)
                lam_ref[c, plane, rows, :] = here
                for place, value in ((plane + 1, here), (other, there)):
                    base = (c * 4 + place) * ROWS
                    at = pl.ds(pl.multiple_of(base + start, 8), 8)
                    x_ref[at, :H] = value[:, :H] + value[:, H:]
                    x_ref[at, H:] = value[:, :H] - value[:, H:]

    for block in range(2):
        lanes = pl.ds(block * H, H)
        out = dot3(x_ref[:, lanes], forward_ref, block)
        for c in range(3):
            for place in range(4):
                base = (c * 4 + place) * ROWS
                for part in range(2):
                    h_ref[block * 2 + part, pl.ds(SUBLANE[c] + place, ROWS, stride=16), :] = out[
                        base : base + ROWS, part * BL : (part + 1) * BL
                    ]

    r = [jnp.broadcast_to(table_ref[R_ROW, :, q * BL : (q + 1) * BL], (16, BL)) for q in range(4)]
    zero = jnp.zeros((16, BL), jnp.float32)

    def ahead(y, carry):
        at = pl.ds(pl.multiple_of(y * 16, 16), 16)
        new = []
        for q in range(4):
            value = h_ref[q, at, :] + r[q] * carry[q]
            u_ref[q, at, :] = value
            new.append(value)
        return tuple(new)

    u_end = lax.fori_loop(0, ROWS, ahead, (zero,) * 4, unroll=8)

    def back(i, carry):
        y = ROWS - 1 - i
        at = pl.ds(pl.multiple_of(y * 16, 16), 16)
        new = [u_ref[q, at, :] + r[q] * carry[q] for q in range(4)]
        return (*new, carry[4] + new[0])

    w_end = lax.fori_loop(0, ROWS, back, (zero,) * 5, unroll=8)
    for q in range(4):
        lanes = pl.ds(q * BL, BL)
        ends_ref[0:8, lanes] = u_end[q][0:8]
        ends_ref[8:12, lanes] = u_end[q][12:16]
        ends_ref[12:20, lanes] = w_end[q][0:8]
        ends_ref[20:24, lanes] = w_end[q][12:16]
    lane = lax.broadcasted_iota(jnp.int32, (16, BL), 1)
    sub = lax.broadcasted_iota(jnp.int32, (16, BL), 0)
    sums = jnp.broadcast_to(w_end[4][:, 0:1], (16, BL))
    ends_ref[24:25, :] = jnp.zeros((1, N), jnp.float32)
    used = (lane == sub) & ((sub < 8) | (sub >= 12))
    ends_ref[24:25, 0:BL] = jnp.sum(jnp.where(used, sums, 0.0), axis=0, keepdims=True)


def first_of(s, lows, far, own_codes, far_codes, forward, table):
    args, tree = jax.tree.flatten((lows, far, own_codes, far_codes, forward, table))

    def body(*refs):
        first_kernel(s, *jax.tree.unflatten(tree, refs[: len(args)]), *refs[len(args) :])

    return pl.pallas_call(
        body,
        out_shape=(
            jax.ShapeDtypeStruct((3, 2, ROWS, N), jnp.float32),
            jax.ShapeDtypeStruct((4, ROWS * 16, BL), jnp.float32),
            jax.ShapeDtypeStruct((25, N), jnp.float32),
        ),
        in_specs=[pl.BlockSpec(memory_space=pltpu.VMEM)] * len(args),
        out_specs=(pl.BlockSpec(memory_space=pltpu.VMEM),) * 3,
        scratch_shapes=[
            pltpu.VMEM((12 * ROWS, N), jnp.float32),
            pltpu.VMEM((4, ROWS * 16, BL), jnp.float32),
        ],
        compiler_params=pltpu.CompilerParams(vmem_limit_bytes=VMEM_LIMIT),
        cost_estimate=pl.CostEstimate(flops=3_000_000_000, bytes_accessed=8_000_000, transcendentals=0),
        name="first",
    )(*args)


def second_kernel(
    zero_u, zero_z, last, *refs
):
    ends_refs = refs[:GROUPS]
    u_ref, lam_ref, omega_ref, table_ref, inverse_ref = refs[GROUPS : GROUPS + 5]
    out_refs = refs[GROUPS + 5 : -2]
    y_ref, field_ref = refs[-2:]
    me = lax.axis_index("pencil")
    u_in = [[jnp.zeros((8, BL), jnp.float32)] * 2 for _ in range(4)]
    w_in = [[jnp.zeros((8, BL), jnp.float32)] * 2 for _ in range(4)]
    u_sum = [jnp.zeros((8, BL), jnp.float32)] * 2
    w_sum = [jnp.zeros((8, BL), jnp.float32)] * 2
    z_row = jnp.zeros((1, BL), jnp.float32)
    for step in range(GROUPS):
        ends_ref = ends_refs[step]
        who = (me ^ step) - me & (GROUPS - 1)
        for q in range(4):
            lanes = pl.ds(q * BL, BL)
            uu = table_ref[CUU_ROW + who, :, lanes]
            ww = table_ref[CWW_ROW + who, :, lanes]
            wu = table_ref[CWU_ROW + who, :, lanes]
            for g in range(2):
                u = ends_ref[4 * g : 4 * g + 8, lanes]
                w = ends_ref[12 + 4 * g : 20 + 4 * g, lanes]
                u_in[q][g] = u_in[q][g] + uu * u
                w_in[q][g] = w_in[q][g] + (ww * w + wu * u)
                if q == 0:
                    u_sum[g] = u_sum[g] + u
                    w_sum[g] = w_sum[g] + w
        z_row = z_row + ends_ref[24:25, 0:BL]
    lane = lax.broadcasted_iota(jnp.int32, (8, BL), 1)
    sub = lax.broadcasted_iota(jnp.int32, (8, BL), 0)
    first_lane = lane == 0
    mean = []
    for g in range(2):
        u_in[0][g] = u_in[0][g] + jnp.where(first_lane, zero_u * w_sum[g], 0.0)
        mean.append(jnp.where(first_lane, u_sum[g] * (1.0 / N), 0.0))
        mine = jnp.where(lane == sub + 8 * g, jnp.broadcast_to(z_row, (8, BL)), 0.0)
        z_total = jnp.broadcast_to(jnp.sum(mine, axis=1, keepdims=True), (8, BL))
        w_in[0][g] = w_in[0][g] + jnp.where(first_lane, zero_z * z_total, 0.0)

    r = [jnp.broadcast_to(table_ref[R_ROW, :, q * BL : (q + 1) * BL], (8, BL)) for q in range(4)]
    swap = [
        jnp.broadcast_to(table_ref[SWAP_ROW, :, q * BL : (q + 1) * BL], (8, BL)) for q in range(4)
    ]
    upper = sub < 4

    def emit(y, after, here, before):
        at = pl.ds(pl.multiple_of(y * 8, 8), 8)
        at_b = pl.ds(pl.multiple_of(ROWS * 8 + y * 8, 8), 8)
        for q in range(4):
            slope0 = 0.5 * (after[2 * q] - before[2 * q])
            slope1 = 0.5 * (after[2 * q + 1] - before[2 * q + 1])
            turned = swap[q] * here[2 * (q ^ 1)]
            lanes = pl.ds(q * BL, BL)
            y_ref[at, lanes] = jnp.where(upper, here[2 * q], slope1 - turned)
            y_ref[at_b, lanes] = slope0

    def back(i, carry):
        y = ROWS - 1 - i
        after, here = carry[:8], carry[8:]
        new = []
        for q in range(4):
            power = table_ref[y, :, q * BL : (q + 1) * BL]
            for g in range(2):
                at = pl.ds(pl.multiple_of(y * 16 + 8 * g, 8), 8)
                value = u_ref[q, at, :] + power * u_in[q][g]
                if q == 0:
                    value = value - (y + 1).astype(jnp.float32) * mean[g]
                new.append(value + r[q] * here[2 * q + g])
        emit(y + 1, after, here, new)
        return (*here, *new)

    edge = tuple(w_in[q][g] for q in range(4) for g in range(2))
    new = []
    for q in range(4):
        power = table_ref[ROWS - 1, :, q * BL : (q + 1) * BL]
        for g in range(2):
            value = u_ref[q, (ROWS - 1) * 16 + 8 * g : (ROWS - 1) * 16 + 8 * g + 8, :]
            value = value + power * u_in[q][g]
            if q == 0:
                value = value - float(ROWS) * mean[g]
            new.append(value + r[q] * edge[2 * q + g])
    carry = lax.fori_loop(1, ROWS, back, (*edge, *new), unroll=3)
    after, here = carry[:8], carry[8:]
    before = [u_in[q][g] + r[q] * here[2 * q + g] for q in range(4) for g in range(2)]
    emit(jnp.int32(0), after, here, before)

    even = dot3(y_ref[:, :H], inverse_ref, 0)
    odd = dot3(y_ref[:, H:], inverse_ref, 1)
    for part in range(2):
        lanes = slice(part * BL, (part + 1) * BL)
        field_ref[part] = even[:, lanes] + odd[:, lanes]
        field_ref[2 + part] = even[:, lanes] - odd[:, lanes]

    @pl.loop(0, ROWS // 8)
    def _(step):
        start = pl.multiple_of(step * 8, 8)
        rows = pl.ds(start, 8)

        def load(base):
            parts = [
                field_ref[q, pl.ds(start * 8 + base, 8, stride=8), :]
                for q in range(4)
            ]
            return jnp.concatenate(parts, axis=1)

        g = []
        for place in range(4):
            psi = load(place)
            gx = load(4 + place)
            gz = -load(ROWS * 8 + place)
            gy = 0.5 * (pltpu.roll(psi, N - 1, 1) - pltpu.roll(psi, 1, 1))
            g.append((gx, gy, gz))
        for plane in range(2):
            here = g[plane + 1]
            w = [omega_ref[c, plane, rows, :] for c in range(3)]
            cross = (
                w[1] * here[2] - w[2] * here[1],
                w[2] * here[0] - w[0] * here[2],
                w[0] * here[1] - w[1] * here[0],
            )
            for c in range(3):
                slope = 0.5 * (g[plane + 2][c] - g[plane][c])
                new = lam_ref[c, plane, rows, :] + TIME_STEP * (cross[c] + w[0] * slope)
                if last:
                    out_refs[0][c, plane, rows, :] = new
                else:
                    out_refs[plane][c, rows, :] = new


def second_of(t, last, *args):
    def body(*refs):
        second_kernel(t["zero_u"], t["zero_z"], last, *refs)

    if last:
        shapes = (jax.ShapeDtypeStruct((3, 2, ROWS, N), jnp.float32),)
    else:
        shapes = (jax.ShapeDtypeStruct((3, ROWS, N), jnp.float32),) * 2
    return pl.pallas_call(
        body,
        out_shape=shapes,
        in_specs=[pl.BlockSpec(memory_space=pltpu.VMEM)] * (GROUPS + 5),
        out_specs=(pl.BlockSpec(memory_space=pltpu.VMEM),) * len(shapes),
        scratch_shapes=[
            pltpu.VMEM((ROWS * 16, N), jnp.float32),
            pltpu.VMEM((4, ROWS * 16, BL), jnp.float32),
        ],
        compiler_params=pltpu.CompilerParams(vmem_limit_bytes=VMEM_LIMIT),
        cost_estimate=pl.CostEstimate(flops=4_000_000_000, bytes_accessed=8_000_000, transcendentals=0),
        name="second",
    )(*args)


def shifted(value, axis, by):
    count = lax.axis_size(axis)
    return lax.ppermute(value, axis, [(i, (i + by) % count) for i in range(count)])


def neighbours(lower_plane, upper_plane):
    below = shifted(upper_plane, "slab", 1)
    above = shifted(lower_plane, "slab", -1)
    return below, above


FAR = ((15, 16), (31, 0))
RELAY_UP = ({15: 12, 31: 28}, {12: 16, 28: 0})
RELAY_DOWN = ({16: 19, 0: 3}, {19: 15, 3: 31})


def relayed(both, singles):
    count = lax.axis_size("slab")
    up = [(i, (i + 1) % count) for i in range(count)]
    sides = (
        (1, [p for p in up if p not in FAR], RELAY_UP),
        (0, [(b, a) for a, b in up if (a, b) not in FAR], RELAY_DOWN),
    )
    out = [[], []]
    for plane, near, relay in sides:
        direct = lax.ppermute(both[plane], "slab", near)
        for s in range(2):
            hop = lax.ppermute(singles[s][plane], "slab", list(relay[0].items()))
            out[s].append((direct, lax.ppermute(hop, "slab", list(relay[1].items()))))
    return out


def crossed(value, mask):
    return lax.ppermute(value, "pencil", [(i, i ^ mask) for i in range(GROUPS)])


def gathered(ends):
    far = [ends] + [crossed(ends, 2 * d) for d in (1, 2, 3)]
    out = []
    for value in far:
        out += [value, crossed(value, 1)]
    return out


def steps(adjoint_vort, omega_ckpt, cell_shift, move_count, move_blocks):
    t = tables()
    forward, inverse = halves(t["forward"]), halves(t["inverse"])
    rows = [t["rpow"], t["cuu"], t["cww"], t["cwu"], t["r"][None], t["swap"][None]]
    table = jnp.asarray(np.concatenate(rows)[:, None], jnp.float32)

    lows = early_of(move_count, move_blocks, cell_shift, adjoint_vort)
    far = neighbours(*lows)
    packed = packed_of(move_count, move_blocks, cell_shift, omega_ckpt)
    far_packed = relayed(packed[0], packed[1:])
    for s in range(2):
        if s == 0:
            own_codes, far_codes = lows, [(value,) for value in far]
            omega = omega_of(s, omega_ckpt, own_codes, far_codes, far_packed[0])
        else:
            far = neighbours(*lows)
            own_codes, far_codes = packed[0], far_packed[1]
            omega = omega_of(s, omega_ckpt, own_codes, far_codes, far_packed[1])
            far, omega = lax.optimization_barrier((far, omega))
        lam_r, u, ends = first_of(s, lows, far, own_codes, far_codes, forward, table)
        out = second_of(t, s == 1, *gathered(ends), u, lam_r, omega, table, inverse)
        if s == 0:
            lows = out
    return out[0]


def solution(mesh):
    return jax.shard_map(
        steps,
        mesh=mesh,
        in_specs=(
            P(None, "slab", "pencil", None),
            P(None, None, "slab", "pencil", None),
            P(None, "slab", "pencil", None),
            P(None, "slab", "pencil", None),
            P(None, "slab", "pencil", None, None),
        ),
        out_specs=P(None, "slab", "pencil", None),
        check_vma=False,
    )
```
